512 devices in a mesh: tm: 64 (over y, z), head: 8 (over x, core).
Axes of the slice: x: 4, y: 4, z: 16, core: 2. Of those that a mesh axis runs over, the one named last changes fastest.
Arguments:
- frames: bfloat16 [16384, 1024], P('tm'), may hold values from -6 to 6
- x_weight: bfloat16 [1024, 2048], P('tm', 'head'), may hold values from -0.1875 to 0.1875
- z_weight: bfloat16 [1024, 2048], P('tm', 'head'), may hold values from -0.1875 to 0.1875
- bc_weight: bfloat16 [1024, 256], P('tm'), may hold values from -0.1875 to 0.1875
- log_decay: float32 [32, 16384], P('head', 'tm'), may hold values from -0.9 to 0
- norm_gain: float32 [2048], P('head'), may hold values from 0.1 to 1.9
- conv_weight: float32 [31, 2048], P(None, 'head'), may hold values from -1 to 1
- out_weight: bfloat16 [2048, 1024], P('head', 'tm'), may hold values from -0.125 to 0.125
- record_lengths: int32 [8], replicated, may hold values from 1 to 12288, 16384 in all
Outputs:
- mixed: bfloat16 [16384, 1024], P('tm', 'head')
The draws below stay inside these ranges and needn't reach their ends.
Inputs may be any that keep to these rules, and one draw needn't show every extreme that they name: `record_lengths`: 8 recording lengths that sum to 16384; the longest has exactly 12288 frames.
All inputs are finite; a program needn't handle non-finite values.
Results may differ from the reference program's by a relative error of at most 0.02.
Values may be sent and summed in bfloat16 or wider, within the bound.
A program may use at most 64 MiB of HBM per device.

```python
import math
import jax
import jax.numpy as jnp
import numpy as np
from jax import lax

D = 1024
SCAN_GROUPS = 32
P_SIZE = 64
N = 128
KCONV = 31
SPAN = 128
NREC = 8
TOK_DEV = 256
PACKED_STEPS = 16384
LONGEST = 12288
HALF = 15
HP = 2048
HP_DEV = 256
N_HEAD = 8


def draw_log_decay(key, part):
    sampler_seeds = [jax.random.fold_in(key, 11 + number) for number in range(8)]
    fast_share = 0.5
    fast = jax.random.bernoulli(sampler_seeds[0], fast_share, (SCAN_GROUPS,))
    fast_rate = jnp.exp(jax.random.uniform(sampler_seeds[1], (SCAN_GROUPS,), jnp.float32, math.log(1.0 / 50.0), math.log(1.0 / 30.0)))
    slow_rate = jnp.exp(jax.random.uniform(sampler_seeds[2], (SCAN_GROUPS,), jnp.float32, math.log(0.3), math.log(1.5))) / PACKED_STEPS
    fading_speed = jnp.where(fast, fast_rate, slow_rate)
    block_count = PACKED_STEPS // TOK_DEV
    tile_factor = jnp.exp(jax.random.uniform(sampler_seeds[3], (SCAN_GROUPS, block_count), jnp.float32, math.log(0.5), math.log(2.0)))
    tile_factor = jnp.repeat(tile_factor, TOK_DEV, axis=1)
    approximate_guess = jnp.exp(jax.random.uniform(sampler_seeds[4], (SCAN_GROUPS, PACKED_STEPS), jnp.float32, math.log(0.5), math.log(2.0)))
    spurt_span = jax.random.bernoulli(sampler_seeds[5], 4.0 / PACKED_STEPS, (SCAN_GROUPS, PACKED_STEPS))
    objective_scalar = jax.random.uniform(sampler_seeds[6], (SCAN_GROUPS, PACKED_STEPS), jnp.float32, 0.2, 0.5)
    return (-(fading_speed[:, None] * tile_factor * approximate_guess) + jnp.where(spurt_span, jnp.log1p(-objective_scalar), 0.0)).astype(jnp.float32)


def steps_of(own_key, extent, split, low, top_value):
    factor_of = 1.0
    for axis_at, parts in split:
        draws = jax.random.uniform(jax.random.fold_in(jax.random.fold_in(own_key, 6), axis_at), (parts,), jnp.float32, low / len(split), top_value / len(split))
        factor_of = factor_of * jnp.repeat(jnp.exp(draws), extent[axis_at] // parts).reshape((-1,) + (1,) * (len(extent) - 1 - axis_at))
    return factor_of


def length_profile(amount, total, most, skew):
    portions = [(1 << 20) // math.isqrt(rank ** skew) + 1 for rank in range(2, amount + 1)]
    surplus, holding = total - most - (amount - 1), [1] * (amount - 1)
    while surplus > 0:
        movable = [i for i in range(amount - 1) if holding[i] < most]
        whole, budget = sum([portions[i] for i in movable]), surplus
        for i in movable:
            addition = min(most - holding[i], max(1, budget * portions[i] // whole), surplus)
            holding[i] = holding[i] + addition
            surplus = surplus - addition
    return np.array([most] + holding)


def uneven(rng, number_of, total, reach, slope):
    if number_of == 2:
        one = jax.random.randint(rng, (), max(1, total - reach), min(reach, total - 1) + 1)
        return jnp.stack([one, total - one])
    tallies = jnp.asarray(length_profile(number_of, total, reach, slope), jnp.int32)
    twos = (number_of - 1) // 2
    source_of, receiver = tallies[1:1 + 2 * twos:2], tallies[2:2 + 2 * twos:2]
    room = jnp.minimum(source_of - 1, reach - receiver)
    shifted = jax.random.randint(jax.random.fold_in(rng, 1), (twos,), 0, 1 << 20) % (room + 1)
    tallies = tallies.at[1:1 + 2 * twos:2].set(source_of - shifted).at[2:2 + 2 * twos:2].set(receiver + shifted)
    return tallies[jax.random.permutation(jax.random.fold_in(rng, 2), number_of)]


def normal_values(rng, dims, scale, bound, split=(), kind=jnp.bfloat16):
    gain = steps_of(rng, dims, split, -0.22, 0.18) if split else 1.0
    drawn = jax.random.normal(rng, dims, jnp.float32) * scale * gain
    return jnp.minimum(jnp.maximum(drawn, -bound), bound).astype(kind)


def setup_inputs(seed: int = 0) -> dict:
    keys = jax.random.split(jax.random.key(seed), 10)
    frames = normal_values(keys[0], (PACKED_STEPS, D), 1.0, 6.0, ((0, 64),))
    x_weight = normal_values(keys[1], (D, HP), D ** -0.5, 0.1875, ((0, 64), (1, 8)))
    z_weight = normal_values(keys[2], (D, HP), D ** -0.5, 0.1875, ((0, 64), (1, 8)))
    bc_weight = normal_values(keys[3], (D, 2 * N), D ** -0.5, 0.1875, ((0, 64),))
    log_decay = draw_log_decay(jax.random.fold_in(keys[9], 71), 0)
    norm_gain = jnp.clip(1.0 + 0.18 * jax.random.normal(keys[5], (HP,), jnp.float32), 0.1, 1.9)
    conv_weight = normal_values(keys[6], (KCONV, HP), KCONV ** -0.5, 1.0, ((1, 8),), jnp.float32)
    out_weight = normal_values(keys[7], (HP, D), HP ** -0.5, 0.125, ((0, 8), (1, 64)))
    record_lengths = uneven(keys[8], NREC, PACKED_STEPS, LONGEST, 2).astype(jnp.int32)
    return dict(frames=frames, x_weight=x_weight, z_weight=z_weight, bc_weight=bc_weight, log_decay=log_decay, norm_gain=norm_gain, conv_weight=conv_weight, out_weight=out_weight, record_lengths=record_lengths)


highest = lax.Precision.HIGHEST

def segment_ids(record_lengths, positions):
    record_ends = jnp.cumsum(record_lengths).astype(jnp.int32)
    return lax.optimization_barrier(jnp.sum((record_ends[None, :] <= positions[:, None]).astype(jnp.int32), axis=1)).astype(jnp.int32)

def span_step(state, inputs):
    x_block, b_block, c_block, log_block, seg_block, seg_before = inputs
    length = seg_block.shape[0]
    cumul = jnp.cumsum(log_block, axis=1)
    lower = jnp.arange(length)[:, None] >= jnp.arange(length)[None, :]
    joined = (seg_block[:, None] == seg_block[None, :]) & lower
    spread = cumul[:, :, None] - cumul[:, None, :]
    mixing = jnp.exp(jnp.where(joined[None], spread, -jnp.inf))
    scores = jnp.dot(c_block, b_block.T, preferred_element_type=jnp.float32)
    x_float = x_block.astype(jnp.float32)
    inner = jnp.einsum('hts,shp->thp', mixing * scores[None], x_float, precision=highest)
    carried = jnp.exp(cumul) * (seg_block == seg_before).astype(jnp.float32)[None, :]
    c_float = c_block.astype(jnp.float32)
    outer = jnp.einsum('tn,hnp->thp', c_float, state, precision=highest) * carried.T[:, :, None]
    tail = jnp.exp(cumul[:, -1:] - cumul) * (seg_block == seg_block[-1]).astype(jnp.float32)[None, :]
    weighted = tail[:, :, None] * b_block.astype(jnp.float32)[None, :, :]
    state_next = carried[:, -1][:, None, None] * state + jnp.einsum('hsn,shp->hnp', weighted, x_float, precision=highest)
    return (state_next, inner + outer)

def run_spans(x_rows, b_rows, c_rows, log_rows, seg_rows, seg_first, state):
    count = x_rows.shape[0] // SPAN
    heads_here = log_rows.shape[0]
    x_blocks = x_rows.reshape(count, SPAN, heads_here, -1)
    b_blocks = b_rows.reshape(count, SPAN, -1)
    c_blocks = c_rows.reshape(count, SPAN, -1)
    log_blocks = log_rows.reshape(heads_here, count, SPAN).transpose(1, 0, 2)
    seg_blocks = seg_rows.reshape(count, SPAN)
    seg_befores = jnp.concatenate([jnp.reshape(seg_first, (1,)).astype(jnp.int32), seg_blocks[:-1, -1].astype(jnp.int32)])
    state, outputs = lax.scan(span_step, state, (x_blocks, b_blocks, c_blocks, log_blocks, seg_blocks, seg_befores))
    return (state, outputs.reshape(count * SPAN, heads_here, -1))

def gate_rows(ssd_out, z_rows, norm_gain):
    square_mean = lax.optimization_barrier(jnp.mean(ssd_out * ssd_out, axis=-1, keepdims=True))
    normed = (ssd_out * lax.rsqrt(square_mean + 1e-05)).reshape(ssd_out.shape[0], -1)
    z_float = z_rows.astype(jnp.float32)
    return (normed * norm_gain[None, :] * z_float * jax.nn.sigmoid(z_float)).astype(jnp.bfloat16)

def conv_rows(extended, seg_extended, seg_rows, conv_weight):
    frame_count = seg_rows.shape[0]
    summed = jnp.zeros((frame_count, extended.shape[1]), jnp.float32)
    for offset in range(conv_weight.shape[0]):
        same = (seg_extended[offset:offset + frame_count] == seg_rows).astype(jnp.float32)
        summed = summed + conv_weight[offset][None, :] * extended[offset:offset + frame_count].astype(jnp.float32) * same[:, None]
    return (summed * jax.nn.sigmoid(summed)).astype(jnp.bfloat16)

def reference(frames, x_weight, z_weight, bc_weight, log_decay, norm_gain, conv_weight, out_weight, record_lengths):
    x_rows = jnp.dot(frames, x_weight, preferred_element_type=jnp.float32).astype(jnp.bfloat16)
    z_rows = jnp.dot(frames, z_weight, preferred_element_type=jnp.float32).astype(jnp.bfloat16)
    bc_rows = jnp.dot(frames, bc_weight, preferred_element_type=jnp.float32).astype(jnp.bfloat16)
    positions = jnp.arange(PACKED_STEPS, dtype=jnp.int32)
    seg_rows = segment_ids(record_lengths, positions)
    start_state = jnp.zeros((SCAN_GROUPS, N, P_SIZE), jnp.float32)
    final_state, ssd_out = run_spans(x_rows, bc_rows[:, :N], bc_rows[:, N:], log_decay, seg_rows, jnp.int32(-1), start_state)
    gated = gate_rows(ssd_out, z_rows, norm_gain)
    extended = jnp.pad(gated, ((HALF, HALF), (0, 0)))
    seg_extended = segment_ids(record_lengths, jnp.arange(PACKED_STEPS + 2 * HALF, dtype=jnp.int32) - HALF)
    act_rows = conv_rows(extended, seg_extended, seg_rows, conv_weight)
    mixed = jnp.zeros((PACKED_STEPS, D), jnp.float32)
    for group in range(N_HEAD):
        lo_row = group * HP_DEV
        partial_sum = jnp.dot(act_rows[:, lo_row:lo_row + HP_DEV], out_weight[lo_row:lo_row + HP_DEV], preferred_element_type=jnp.float32)
        rounded = lax.optimization_barrier(partial_sum.astype(jnp.bfloat16))
        mixed = mixed + rounded.astype(jnp.float32)
    return mixed.astype(jnp.bfloat16)
```

```python
import functools

import jax
import jax.numpy as jnp
from jax import lax
from jax.experimental import pallas as pl
from jax.experimental.pallas import tpu as pltpu
from jax.sharding import PartitionSpec as P

NY = 4
MESH = pl.DeviceIdType.MESH
HIGHEST = lax.Precision.HIGHEST
F32 = jnp.float32
BF16 = jnp.bfloat16
PS = 64


def nt(a, b, **kw):
    return lax.dot_general(a, b, (((1,), (1,)), ((), ())), preferred_element_type=F32, **kw)


def tn(a, b, **kw):
    return lax.dot_general(a, b, (((0,), (0,)), ((), ())), preferred_element_type=F32, **kw)


def nn(a, b, **kw):
    return jnp.dot(a, b, preferred_element_type=F32, **kw)


def iota(shape, dim):
    return lax.broadcasted_iota(jnp.int32, shape, dim)


def kernel(
    ny, nz, nx,
    lens, frames, xw, zw, bcw, logd, gain, convw, outw, out,
    ga, gb, mix, growth, tail, wm, xs, bcs, inner, zs, local, got, keeps, keep_own,
    pref, ckeep, tot, tots, back, entry, gated, ext, halo_lo, halo_hi, act,
    part, pair, red, redin,
    s_loc, s_ay, r_ay, s_az, r_az, s_bz, r_bz, s_by, r_by,
    s_k, r_k, s_s, r_s, s_t, r_t, s_p, r_p, s_h, r_h, s_c, r_c, s_x, r_x,
):
    me, hd = lax.axis_index("tm"), lax.axis_index("head")
    y, z = lax.div(me, nz), lax.rem(me, nz)
    x, core = lax.div(hd, 2), lax.rem(hd, 2)
    rows, depth, chans = frames.shape[0], xw.shape[0], xw.shape[1]
    width = frames.shape[1]
    heads = chans // PS
    states = bcw.shape[1] // 2
    taps = convw.shape[0]
    half = (taps - 1) // 2
    far = nz // 2
    base = me * rows

    def at(yy, zz):
        return {"tm": yy * nz + zz}

    def turn(a, d, n):
        return lax.rem(a + d + n, n)

    pending = []

    def send(src, dst, ssem, rsem, dev):
        copy = pltpu.make_async_remote_copy(
            src_ref=src, dst_ref=dst, send_sem=ssem, recv_sem=rsem,
            device_id=dev, device_id_type=MESH,
        )
        copy.start()
        pending.append(copy)

    def recv(dst, rsem):
        pltpu.make_async_copy(dst, dst, rsem).wait()

    own = [
        pltpu.make_async_copy(xw, ga.at[0, y, z], s_loc.at[0]),
        pltpu.make_async_copy(bcw, ga.at[1, y, z], s_loc.at[1]),
        pltpu.make_async_copy(zw, gb.at[0, y, z], s_loc.at[2]),
    ]
    for copy in own:
        copy.start()
    barrier = pltpu.get_barrier_semaphore()
    greet = [at(turn(y, d, ny), z) for d in range(1, ny)]
    greet += [at(y, turn(z, 1, nz)), at(y, turn(z, -1, nz))]
    greet += [{"head": 2 * x + 1 - core}]
    greet += [{"head": 2 * turn(x, d, nx) + core} for d in range(1, nx)]
    for dev in greet:
        pl.semaphore_signal(barrier, inc=1, device_id=dev, device_id_type=MESH)
    eye = (iota((depth, depth), 0) == iota((depth, depth), 1)).astype(BF16)
    gb[1, y, z] = nt(eye, outw[...]).astype(BF16)
    for copy in own:
        copy.wait()
    pl.semaphore_wait(barrier, len(greet))

    def fwd_a(way, step, d):
        yy, zz = turn(y, -d, ny), turn(z, -step if way == 0 else step, nz)
        ref = ga.at[:, yy, zz]
        send(ref, ref, s_az.at[way, step, d], r_az.at[way, step + 1, d],
             at(y, turn(z, 1 if way == 0 else -1, nz)))

    def takes_a(way, step, d):
        return step < far or (step == far and (d < ny // 2) == (way == 0))

    def ref_b(way, step):
        zz = turn(z, -step if way == 0 else step, nz)
        return gb.at[:, y, zz] if step < far else gb.at[pl.ds(way, 1), y, zz]

    def fwd_b(way, step):
        zz = turn(z, -step if way == 0 else step, nz)
        ref = gb.at[:, y, zz] if step + 1 < far else gb.at[pl.ds(way, 1), y, zz]
        send(ref, ref, s_bz.at[way, step], r_bz.at[way, step + 1],
             at(y, turn(z, 1 if way == 0 else -1, nz)))

    for way in (0, 1):
        if takes_a(way, 1, 0):
            fwd_a(way, 0, 0)
    for d in range(1, ny):
        ref = ga.at[:, y, z]
        send(ref, ref, s_ay.at[d - 1], r_ay.at[d - 1], at(turn(y, d, ny), z))
    for way in (0, 1):
        fwd_b(way, 0)

    ends = []
    total = jnp.int32(0)
    for r in range(lens.shape[0]):
        total = total + lens[r]
        ends.append(total)
    pos = base + iota((rows, 1), 0)
    start = jnp.zeros((rows, 1), jnp.int32)
    for e in ends:
        start = jnp.where(pos >= e, e, start)
    stop = jnp.full((rows, 1), ends[-1], jnp.int32)
    for e in reversed(ends):
        stop = jnp.where(pos < e, e, stop)
    vals = {}

    def piece_cumul():
        low = iota((rows, rows), 0) >= iota((rows, rows), 1)
        tril = low.astype(F32)
        spread = jnp.concatenate(
            [jnp.broadcast_to(logd[h : h + 1, :], (PS, rows)) for h in range(heads)], axis=0
        )
        cum = nt(tril, spread, precision=HIGHEST)
        vals["cum"] = cum
        vals["row"] = nt(logd[...], tril, precision=HIGHEST)
        last = cum[rows - 1 : rows, :]
        last_start = start[rows - 1 : rows, :]
        growth[...] = jnp.where(start < base, jnp.exp(cum), 0.0)
        tail[...] = jnp.where(pos >= last_start, jnp.exp(last - cum), 0.0)
        keep_own[...] = jnp.where(last_start < base, jnp.exp(last), 0.0)

    def piece_mix(h):
        low = iota((rows, rows), 0) >= iota((rows, rows), 1)
        joined = low & (base + iota((rows, rows), 1) >= start)
        diff = vals["cum"][:, h * PS : h * PS + 1] - vals["row"][h : h + 1, :]
        mix[h] = jnp.exp(jnp.where(joined, diff, -1e30))

    def piece_taps(k_lo, k_hi):
        lanes = 128
        before = jnp.broadcast_to(start - pos, (rows, lanes))
        after = jnp.broadcast_to(stop - pos, (rows, lanes))
        for k in range(k_lo, k_hi):
            ok = (k - half >= before) if k <= half else (k - half < after)
            for lo in range(0, chans, lanes):
                wm[k, :, lo : lo + lanes] = jnp.where(ok, convw[k : k + 1, lo : lo + lanes], 0.0)

    pieces = [piece_cumul]
    pieces += [functools.partial(piece_mix, h) for h in range(heads)]
    pieces += [
        functools.partial(piece_taps, k, min(k + 4, taps)) for k in range(0, taps, 4)
    ]
    pieces[0]()
    pieces.pop(0)
    per_step = -(-len(pieces) // far)

    for d in range(1, ny):
        recv(ga.at[:, turn(y, -d, ny), z], r_ay.at[d - 1])
        for way in (0, 1):
            if takes_a(way, 1, d):
                fwd_a(way, 0, d)
    for step in range(1, far + 1):
        for piece in pieces[:per_step]:
            piece()
        pieces = pieces[per_step:]
        for d in range(ny):
            for way in (0, 1):
                if takes_a(way, step, d):
                    zz = turn(z, -step if way == 0 else step, nz)
                    recv(ga.at[:, turn(y, -d, ny), zz], r_az.at[way, step, d])
                    if takes_a(way, step + 1, d):
                        fwd_a(way, step, d)
        for way in (0, 1):
            recv(ref_b(way, step), r_bz.at[way, step])
            if step < far:
                fwd_b(way, step)

    for plane in (0, 1):
        for d in range(1, ny):
            ref = gb.at[plane, y]
            send(ref, ref, s_by.at[plane, d - 1], r_by.at[plane, d - 1], at(turn(y, d, ny), z))

    keeps[z] = keep_own[...]
    for d in range(1, nz):
        send(keep_own, keeps.at[z], s_k.at[d], r_k.at[d], at(y, turn(z, d, nz)))

    bc = nn(frames[...], ga[1].reshape(width, chans)).astype(BF16)
    bcs[...] = bc
    xr = nn(frames[...], ga[0].reshape(width, chans))
    xb = xr.astype(BF16)
    xs[...] = xb
    weighted = (xb.astype(F32) * tail[...]).astype(BF16)
    state = tn(bcs[:, :states], weighted).astype(BF16)
    share = local.shape[1]
    for lo in range(0, chans // 128):
        local[lo * (nz * 128 // chans) : (lo + 1) * (nz * 128 // chans)] = state[
            :, lo * 128 : lo * 128 + 128
        ].reshape(nz * 128 // chans, share, 128)
    for d in range(1, nz):
        zz = turn(z, d, nz)
        send(local.at[zz], got.at[z], s_s.at[d], r_s.at[d], at(y, zz))
    got[z] = local[z]

    scores = nt(bcs[:, states:], bcs[:, :states])
    lane_head = lax.div(iota((rows, chans), 1), PS)
    acc = jnp.zeros((rows, chans), F32)
    for h in range(heads):
        only = jnp.where(lane_head == h, xs[...].astype(F32), 0.0).astype(BF16)
        acc = acc + nn((mix[h] * scores).astype(BF16), only)
    inner[...] = acc

    for d in range(1, nz):
        zz = turn(z, -d, nz)
        recv(keeps.at[zz], r_k.at[d])
        recv(got.at[zz], r_s.at[d])
    carry = jnp.zeros((share, 128), F32)
    decay = jnp.ones((1, 128), F32)
    upper = z >= far
    for zz in range(nz):
        pref[zz] = carry
        ckeep[zz] = decay
        line = keeps[zz]
        keep = line[:, 0:128]
        for lo in range(1, chans // 128):
            keep = jnp.where(lax.div(z, nz * 128 // chans) == lo, line[:, lo * 128 : lo * 128 + 128], keep)
        carry = carry * keep + got[zz].astype(F32)
        decay = decay * keep
    tot[0:share] = carry
    tot[share : share + 8] = jnp.broadcast_to(decay, (8, 128))
    for d in range(1, ny):
        send(tot, tots.at[d - 1], s_t.at[d - 1], r_t.at[d - 1], at(turn(y, d, ny), z))
    for d in range(1, ny):
        recv(tots.at[d - 1], r_t.at[d - 1])
    come = jnp.zeros((share, 128), F32)
    for d in range(ny - 1, 0, -1):
        new = come * tots[d - 1, share : share + 1] + tots[d - 1, 0:share]
        come = jnp.where(y >= d, new, 0.0)
    for zz in range(nz):
        back[zz] = (pref[zz] + ckeep[zz] * come).astype(BF16)
    for d in range(1, nz):
        zz = turn(z, d, nz)
        send(back.at[zz], entry.at[z], s_p.at[d], r_p.at[d], at(y, zz))
    entry[z] = back[z]

    for d in range(1, ny):
        recv(gb.at[0, turn(y, -d, ny)], r_by.at[0, d - 1])
    zr = nn(frames[...], gb[0].reshape(width, chans)).astype(BF16).astype(F32)
    zs[...] = zr * jax.nn.sigmoid(zr) * gain[...]

    for d in range(1, nz):
        recv(entry.at[turn(z, -d, nz)], r_p.at[d])
    each = nz * 128 // chans
    carried = jnp.concatenate(
        [
            nn(bcs[:, states:], entry[lo * each : (lo + 1) * each].reshape(states, 128))
            for lo in range(chans // 128)
        ],
        axis=1,
    )
    ssd = inner[...] + carried * growth[...]
    same = lax.div(iota((chans, chans), 0), PS) == lax.div(iota((chans, chans), 1), PS)
    mean = nn((ssd * ssd).astype(BF16), jnp.where(same, 1.0 / PS, 0.0).astype(BF16))
    g = (ssd * lax.rsqrt(mean + 1e-05) * zs[...]).astype(BF16)
    gated[...] = g
    tms = ny * nz
    send(gated.at[pl.ds(rows - 16, 16)], halo_lo, s_h.at[0], r_h.at[0], {"tm": turn(me, 1, tms)})
    send(gated.at[pl.ds(0, 16)], halo_hi, s_h.at[1], r_h.at[1], {"tm": turn(me, -1, tms)})
    ext[16 : 16 + rows] = g.astype(F32)

    def conv(lo, hi):
        acc = jnp.zeros((hi - lo, chans), F32)
        for k in range(taps):
            off = 16 - half + k
            acc = acc + wm[k, lo:hi, :] * ext[lo + off : hi + off, :]
        act[lo:hi] = (acc * jax.nn.sigmoid(acc)).astype(BF16)

    for lo in range(16, rows - 16, 32):
        conv(lo, min(lo + 32, rows - 16))
    recv(halo_lo, r_h.at[0])
    recv(halo_hi, r_h.at[1])
    ext[0:16] = halo_lo[...].astype(F32)
    ext[16 + rows : 32 + rows] = halo_hi[...].astype(F32)
    conv(0, 16)
    conv(rows - 16, rows)

    for d in range(1, ny):
        recv(gb.at[1, turn(y, -d, ny)], r_by.at[1, d - 1])
    cols = width // (2 * nx)
    per = depth
    for j in range(2 * nx):
        ww = gb[1].reshape(width, chans)[j * cols : (j + 1) * cols]
        part[j // 2, j % 2] = nt(act[...], ww).astype(BF16)
    send(part.at[:, 1 - core], pair, s_c.at[0], r_c.at[0], {"head": 2 * x + 1 - core})
    recv(pair, r_c.at[0])
    for d in range(nx - 1, 0, -1):
        xx = turn(x, d, nx)
        red[d - 1] = (part[xx, core].astype(F32) + pair[xx].astype(F32)).astype(BF16)
        send(red.at[d - 1], redin.at[d - 1], s_x.at[d - 1], r_x.at[d - 1], {"head": 2 * xx + core})
    res = part[x, core].astype(F32) + pair[x].astype(F32)
    for d in range(1, nx):
        recv(redin.at[d - 1], r_x.at[d - 1])
        res = res + redin[d - 1].astype(F32)
    out[...] = res.astype(BF16)
    for copy in pending:
        copy.wait_send()


def solution(mesh):
    tms, groups = mesh.shape["tm"], mesh.shape["head"]
    ny, nz, nx = NY, tms // NY, groups // 2

    def local(frames, xw, zw, bcw, logd, gain, convw, outw, lens):
        rows, width = frames.shape
        depth, chans = xw.shape
        states = bcw.shape[1] // 2
        heads = logd.shape[0]
        taps = convw.shape[0]
        share = states * chans // (nz * 128)
        cols = width // groups
        dma = pltpu.SemaphoreType.DMA
        v = pltpu.VMEM
        far = nz // 2
        scratch = [
            v((2, ny, nz, depth, chans), BF16),
            v((2, ny, nz, depth, chans), BF16),
            v((heads, rows, rows), F32),
            v((rows, chans), F32),
            v((rows, chans), F32),
            v((taps, rows, chans), F32),
            v((rows, chans), BF16),
            v((rows, 2 * states), BF16),
            v((rows, chans), F32),
            v((rows, chans), F32),
            v((nz, share, 128), BF16),
            v((nz, share, 128), BF16),
            v((nz, 1, chans), F32),
            v((1, chans), F32),
            v((nz, share, 128), F32),
            v((nz, 1, 128), F32),
            v((share + 8, 128), F32),
            v((ny - 1, share + 8, 128), F32),
            v((nz, share, 128), BF16),
            v((nz, share, 128), BF16),
            v((rows, chans), BF16),
            v((rows + 32, chans), F32),
            v((16, chans), BF16),
            v((16, chans), BF16),
            v((rows, chans), BF16),
            v((nx, 2, rows, cols), BF16),
            v((nx, rows, cols), BF16),
            v((max(nx - 1, 1), rows, cols), BF16),
            v((max(nx - 1, 1), rows, cols), BF16),
            dma((3,)),
            dma((ny - 1,)), dma((ny - 1,)),
            dma((2, far + 1, ny)), dma((2, far + 1, ny)),
            dma((2, far + 1)), dma((2, far + 1)),
            dma((2, ny - 1)), dma((2, ny - 1)),
            dma((nz,)), dma((nz,)),
            dma((nz,)), dma((nz,)),
            dma((ny - 1,)), dma((ny - 1,)),
            dma((nz,)), dma((nz,)),
            dma((2,)), dma((2,)),
            dma((1,)), dma((1,)),
            dma((max(nx - 1, 1),)), dma((max(nx - 1, 1),)),
        ]
        vm = pl.BlockSpec(memory_space=pltpu.VMEM)
        return pl.pallas_call(
            functools.partial(kernel, ny, nz, nx),
            out_shape=jax.ShapeDtypeStruct((rows, cols), BF16),
            in_specs=[pl.BlockSpec(memory_space=pltpu.SMEM)] + [vm] * 8,
            out_specs=vm,
            scratch_shapes=scratch,
            compiler_params=pltpu.CompilerParams(
                collective_id=0, has_side_effects=True, vmem_limit_bytes=60 * 2**20
            ),
            name="mixer",
        )(lens, frames, xw, zw, bcw, logd, gain.reshape(1, chans), convw, outw)

    in_specs = (
        P("tm", None), P("tm", "head"), P("tm", "head"), P("tm", None), P("head", "tm"),
        P("head"), P(None, "head"), P("head", "tm"), P(),
    )
    return jax.shard_map(
        local, mesh=mesh, in_specs=in_specs, out_specs=P("tm", "head"), check_vma=False
    )
```

```python
import functools

import jax
import jax.numpy as jnp
from jax import lax
from jax.experimental import pallas as pl
from jax.experimental.pallas import tpu as pltpu
from jax.sharding import PartitionSpec as P

NY = 4
EDGE = 16
MESH = pl.DeviceIdType.MESH
HIGHEST = lax.Precision.HIGHEST
F32 = jnp.float32
BF16 = jnp.bfloat16
PS = 64


def nt(a, b, **kw):
    return lax.dot_general(a, b, (((1,), (1,)), ((), ())), preferred_element_type=F32, **kw)


def tn(a, b, **kw):
    return lax.dot_general(a, b, (((0,), (0,)), ((), ())), preferred_element_type=F32, **kw)


def nn(a, b, **kw):
    return jnp.dot(a, b, preferred_element_type=F32, **kw)


def iota(shape, dim):
    return lax.broadcasted_iota(jnp.int32, shape, dim)


def kernel(
    ny, nz, nx, parts,
    lens, frames_in, xw, zw, bcw, logd_in, gain_in, convw_in, outw, out,
    w, frames, logd, gain, convw, mix, growth, tail, wm, xs, bs, cs, inner, zs,
    local, got, keeps, keep_own, pref, ckeep, tot, tots, back, entry, ext, act,
    part, pair, red, redin,
    s_loc, s_a1, r_a1, s_a2, r_a2, s_ay, r_ay, s_b1, r_b1, s_b2, r_b2, s_by, r_by,
    s_f, r_f, s_l, r_l, s_k, r_k, s_s, r_s, s_t, r_t, s_p, r_p, s_c, r_c, s_x, r_x,
):
    me, hd = lax.axis_index("tm"), lax.axis_index("head")
    y, z = lax.div(me, nz), lax.rem(me, nz)
    x, core = lax.div(hd, 2), lax.rem(hd, 2)
    tms = ny * nz
    rows, width = frames_in.shape
    depth, chans = xw.shape
    wide = rows + 2 * EDGE
    heads = chans // PS
    states = bcw.shape[1] // 2
    taps = convw_in.shape[0]
    half = (taps - 1) // 2
    reach = nz // 4
    base = me * rows
    first = base - EDGE

    def at(yy, zz):
        return {"tm": yy * nz + zz}

    def turn(a, d, n):
        return lax.rem(a + d + n, n)

    pending = []

    def send(src, dst, ssem, rsem, dev):
        copy = pltpu.make_async_remote_copy(
            src_ref=src, dst_ref=dst, send_sem=ssem, recv_sem=rsem,
            device_id=dev, device_id_type=MESH,
        )
        copy.start()
        pending.append(copy)

    def recv(dst, rsem):
        pltpu.make_async_copy(dst, dst, rsem).wait()

    barrier = pltpu.get_barrier_semaphore()
    greet = [at(y, turn(z, s * k, nz)) for k in range(reach, 0, -1) for s in (1, -1)]
    greet += [at(turn(y, d, ny), z) for d in range(1, ny)]
    greet += [{"tm": turn(me, 1, tms)}, {"tm": turn(me, -1, tms)}]
    greet += [{"head": 2 * turn(x, d, nx) + core} for d in range(1, nx)]
    greet += [{"head": 2 * x + 1 - core}]
    for dev in greet:
        pl.semaphore_signal(barrier, inc=1, device_id=dev, device_id_type=MESH)

    tiles = [(xw, 0), (xw, 128), (bcw, 0), (bcw, 128), (zw, 0), (zw, 128), (outw, 0), (outw, 128)]
    own = [
        pltpu.make_async_copy(src.at[:, lo : lo + 128], w.at[y, z, i], s_loc.at[i])
        for i, (src, lo) in enumerate(tiles)
    ]
    own.append(pltpu.make_async_copy(logd_in, logd.at[1], s_loc.at[8]))
    own.append(pltpu.make_async_copy(frames_in, frames.at[EDGE : EDGE + rows], s_loc.at[9]))
    own.append(pltpu.make_async_copy(gain_in, gain, s_loc.at[10]))
    own.append(pltpu.make_async_copy(convw_in, convw, s_loc.at[11]))
    for copy in own:
        copy.start()
    for copy in own:
        copy.wait()
    pl.semaphore_wait(barrier, len(greet))

    crit, rest = slice(0, 3), slice(3, 8)

    def stage_1(cut, ssem, rsem):
        ref = w.at[y, z, cut]
        for k in range(reach, 0, -1):
            for way, s in ((0, 1), (1, -1)):
                send(ref, ref, ssem.at[way, k], rsem.at[way, k], at(y, turn(z, s * k, nz)))

    def stage_2(cut, ssem, rsem, way):
        s = 1 - 2 * way
        ref = w.at[y, turn(z, -s * reach, nz), cut]
        for j in range(reach - way, 0, -1):
            send(ref, ref, ssem.at[way, j], rsem.at[way, j], at(y, turn(z, s * j, nz)))

    def cross(off):
        zz = turn(z, -off, nz)
        ref = w.at[y, zz, crit]
        for d in range(1, ny):
            send(ref, ref, s_ay.at[off % nz, d], r_ay.at[off % nz, d], at(turn(y, d, ny), z))

    def got_1(cut, rsem, way, k):
        recv(w.at[y, turn(z, k if way else -k, nz), cut], rsem.at[way, k])

    def got_2(cut, rsem, way, j):
        far = reach + j
        recv(w.at[y, turn(z, far if way else -far, nz), cut], rsem.at[way, j])

    stage_1(crit, s_a1, r_a1)
    cross(0)
    for i, d in enumerate((1, -1)):
        send(logd.at[1], logd.at[1 - d], s_l.at[i], r_l.at[i], {"tm": turn(me, d, tms)})
    send(frames.at[rows : rows + EDGE], frames.at[0:EDGE],
         s_f.at[0], r_f.at[0], {"tm": turn(me, 1, tms)})
    send(frames.at[EDGE : 2 * EDGE], frames.at[rows + EDGE : wide],
         s_f.at[1], r_f.at[1], {"tm": turn(me, -1, tms)})

    ends = []
    total = jnp.int32(0)
    for r in range(lens.shape[0]):
        total = total + lens[r]
        ends.append(total)

    def starts(pos):
        start = jnp.zeros(pos.shape, jnp.int32)
        for e in ends:
            start = jnp.where(pos >= e, e, start)
        return start

    pos = first + iota((wide, 1), 0)
    start = starts(pos)
    vals = {}

    def piece_cumul():
        i, j = iota((wide, rows), 0), iota((wide, rows), 1)
        cols = (
            (j >= rows - EDGE) & (j - (rows - EDGE) <= i),
            j + EDGE <= i,
            (j < EDGE) & (j + EDGE + rows <= i),
        )
        cum, line = 0.0, 0.0
        for p, col in enumerate(cols):
            ones = col.astype(F32)
            lines = logd[p]
            spread = jnp.concatenate(
                [jnp.broadcast_to(lines[h : h + 1, :], (PS, rows)) for h in range(heads)], axis=0
            )
            cum = cum + nt(ones, spread, precision=HIGHEST)
            line = line + nt(lines, ones, precision=HIGHEST)
        vals["cum"], vals["line"] = cum, line
        last = cum[rows - 1 : rows, :]
        last_start = start[rows - 1 : rows, :]
        growth[...] = jnp.where(start < first, jnp.exp(cum), 0.0)
        tail[...] = jnp.where(pos[0:rows] >= last_start, jnp.exp(last - cum[0:rows]), 0.0)
        keep_own[...] = jnp.where(last_start < first, jnp.exp(last), 0.0)

    def piece_mix(h):
        i, j = iota((wide, wide), 0), iota((wide, wide), 1)
        joined = (i >= j) & (first + j >= start)
        diff = vals["cum"][:, h * PS : h * PS + 1] - vals["line"][h : h + 1, :]
        mix[h] = jnp.exp(jnp.where(joined, diff, -1e30))

    def piece_taps(k_lo, k_hi):
        lanes = 128
        here = pos[EDGE : EDGE + rows]
        stop = jnp.full(here.shape, ends[-1], jnp.int32)
        for e in reversed(ends):
            stop = jnp.where(here < e, e, stop)
        before = jnp.broadcast_to(start[EDGE : EDGE + rows] - here, (rows, lanes))
        after = jnp.broadcast_to(stop - here, (rows, lanes))
        for k in range(k_lo, k_hi):
            ok = (k - half >= before) if k <= half else (k - half < after)
            for lo in range(0, chans, lanes):
                wm[k, :, lo : lo + lanes] = jnp.where(ok, convw[k : k + 1, lo : lo + lanes], 0.0)

    for way in (0, 1):
        got_1(crit, r_a1, way, reach)
        stage_2(crit, s_a2, r_a2, way)
    stage_1(rest, s_b1, r_b1)
    for k in range(reach, 0, -1):
        for way in (0, 1):
            if k < reach:
                got_1(crit, r_a1, way, k)
            cross(k if way == 0 else -k)
    recv(logd.at[0], r_l.at[0])
    recv(logd.at[2], r_l.at[1])
    piece_cumul()
    for j in range(1, reach + 1):
        for way in (0, 1):
            if j <= reach - way:
                got_2(crit, r_a2, way, j)
                cross(reach + j if way == 0 else -(reach + j))
    for way in (0, 1):
        got_1(rest, r_b1, way, reach)
        stage_2(rest, s_b2, r_b2, way)
    keeps[z] = keep_own[...]
    for d in range(1, nz):
        send(keep_own, keeps.at[z], s_k.at[d], r_k.at[d], at(y, turn(z, d, nz)))
    for h in range(heads):
        piece_mix(h)
    for off in range(nz):
        for d in range(1, ny):
            recv(w.at[turn(y, -d, ny), turn(z, -off, nz), crit], r_ay.at[off, d])

    recv(frames.at[0:EDGE], r_f.at[0])
    recv(frames.at[rows + EDGE : wide], r_f.at[1])

    def weight(lo, count):
        return jnp.concatenate(
            [w[:, :, lo + i].reshape(width, 128) for i in range(count)], axis=1
        )

    bs[...] = nn(frames[...], weight(2, 1)).astype(BF16)
    xb = nn(frames[...], weight(0, 2)).astype(BF16)
    xs[...] = xb
    weighted = (xb[0:rows].astype(F32) * tail[...]).astype(BF16)
    state = tn(bs[0:rows], weighted).astype(BF16)
    share = local.shape[1]
    each = nz * 128 // chans
    for lo in range(chans // 128):
        local[lo * each : (lo + 1) * each] = state[:, lo * 128 : lo * 128 + 128].reshape(
            each, share, 128
        )
    for d in range(1, nz):
        zz = turn(z, d, nz)
        send(local.at[zz], got.at[z], s_s.at[d], r_s.at[d], at(y, zz))
    got[z] = local[z]

    for way in (0, 1):
        for k in range(1, reach):
            got_1(rest, r_b1, way, k)
        for j in range(1, reach + 1 - way):
            got_2(rest, r_b2, way, j)
    planes = ((0, slice(3, 4)), (1, slice(4, 6)), (2, slice(6, 8)))

    def cross_plane(n):
        ref = w.at[y, :, planes[n][1]]
        for d in range(1, ny):
            send(ref, ref, s_by.at[n, d], r_by.at[n, d], at(turn(y, d, ny), z))

    def got_plane(n):
        for d in range(1, ny):
            recv(w.at[turn(y, -d, ny), :, planes[n][1]], r_by.at[n, d])

    cross_plane(0)
    cross_plane(1)
    for k in range(0, taps, 4):
        piece_taps(k, min(k + 4, taps))

    for d in range(1, nz):
        zz = turn(z, -d, nz)
        recv(keeps.at[zz], r_k.at[d])
        recv(got.at[zz], r_s.at[d])
    carry = jnp.zeros((share, 128), F32)
    decay = jnp.ones((1, 128), F32)
    for zz in range(nz):
        pref[zz] = carry
        ckeep[zz] = decay
        line = keeps[zz]
        keep = line[:, 0:128]
        for lo in range(1, chans // 128):
            keep = jnp.where(lax.div(z, each) == lo, line[:, lo * 128 : lo * 128 + 128], keep)
        carry = carry * keep + got[zz].astype(F32)
        decay = decay * keep
    tot[0:share] = carry
    tot[share : share + 8] = jnp.broadcast_to(decay, (8, 128))
    for d in range(1, ny):
        send(tot, tots.at[d - 1], s_t.at[d - 1], r_t.at[d - 1], at(turn(y, d, ny), z))
    cross_plane(2)
    for d in range(1, ny):
        recv(tots.at[d - 1], r_t.at[d - 1])
    come = jnp.zeros((share, 128), F32)
    for d in range(ny - 1, 0, -1):
        new = come * tots[d - 1, share : share + 1] + tots[d - 1, 0:share]
        come = jnp.where(y >= d, new, 0.0)
    for zz in range(nz):
        back[zz] = (pref[zz] + ckeep[zz] * come).astype(BF16)
    for d in range(1, nz):
        zz = turn(z, d, nz)
        send(back.at[zz], entry.at[z], s_p.at[d], r_p.at[d], at(y, zz))
    entry[z] = back[z]

    got_plane(0)
    cs[...] = nn(frames[...], weight(3, 1)).astype(BF16)
    scores = nt(cs[...], bs[...])
    lane_head = lax.div(iota((wide, chans), 1), PS)
    acc = jnp.zeros((wide, chans), F32)
    for h in range(heads):
        only = jnp.where(lane_head == h, xs[...].astype(F32), 0.0).astype(BF16)
        acc = acc + nn((mix[h] * scores).astype(BF16), only)
    inner[...] = acc
    got_plane(1)
    zr = nn(frames[...], weight(4, 2)).astype(BF16).astype(F32)
    zs[...] = zr * jax.nn.sigmoid(zr) * gain[...]
    same = lax.div(iota((chans, chans), 0), PS) == lax.div(iota((chans, chans), 1), PS)
    block = jnp.where(same, 1.0 / PS, 0.0).astype(BF16)
    got_plane(2)

    for d in range(1, nz):
        recv(entry.at[turn(z, -d, nz)], r_p.at[d])
    come_in = jnp.concatenate(
        [entry[lo * each : (lo + 1) * each].reshape(states, 128) for lo in range(chans // 128)],
        axis=1,
    )
    ssd = inner[...] + nn(cs[...], come_in) * growth[...]
    mean = nn((ssd * ssd).astype(BF16), block)
    g = (ssd * lax.rsqrt(mean + 1e-05) * zs[...]).astype(BF16)
    ext[...] = g.astype(F32)

    cols = width // (2 * nx)
    span = rows // parts
    per = cols // depth

    def conv(lo, hi):
        acc = jnp.zeros((hi - lo, chans), F32)
        for k in range(taps):
            off = EDGE - half + k
            acc = acc + wm[k, lo:hi, :] * ext[lo + off : hi + off, :]
        act[lo:hi] = (acc * jax.nn.sigmoid(acc)).astype(BF16)

    ow = weight(6, 2)
    for p in range(parts):
        for lo in range(p * span, (p + 1) * span, 32):
            conv(lo, lo + 32)
        rows_p = act[p * span : (p + 1) * span]
        for j in range(2 * nx):
            part[p, j // 2, j % 2] = nt(rows_p, ow[j * cols : (j + 1) * cols]).astype(BF16)
        send(part.at[p, :, 1 - core], pair.at[p], s_c.at[p], r_c.at[p], {"head": 2 * x + 1 - core})
    for p in range(parts):
        recv(pair.at[p], r_c.at[p])
        for d in range(nx - 1, 0, -1):
            xx = turn(x, d, nx)
            red[p, d - 1] = (part[p, xx, core].astype(F32) + pair[p, xx].astype(F32)).astype(BF16)
            send(red.at[p, d - 1], redin.at[p, d - 1], s_x.at[p, d - 1], r_x.at[p, d - 1],
                 {"head": 2 * xx + core})
    for p in range(parts):
        res = part[p, x, core].astype(F32) + pair[p, x].astype(F32)
        for d in range(1, nx):
            recv(redin.at[p, d - 1], r_x.at[p, d - 1])
            res = res + redin[p, d - 1].astype(F32)
        out[p * span : (p + 1) * span] = res.astype(BF16)
    for copy in pending:
        copy.wait_send()


def solution(mesh):
    tms, groups = mesh.shape["tm"], mesh.shape["head"]
    ny, nz, nx = NY, tms // NY, groups // 2

    def local(frames, xw, zw, bcw, logd, gain, convw, outw, lens):
        rows, width = frames.shape
        depth, chans = xw.shape
        states = bcw.shape[1] // 2
        heads = logd.shape[0]
        taps = convw.shape[0]
        share = states * chans // (nz * 128)
        cols = width // groups
        wide = rows + 2 * EDGE
        parts = 2
        dma = pltpu.SemaphoreType.DMA
        v = pltpu.VMEM
        reach = nz // 4
        others = max(nx - 1, 1)
        scratch = [
            v((ny, nz, 8, depth, 128), BF16),
            v((wide, width), BF16),
            v((3, heads, rows), F32),
            v((1, chans), F32),
            v((taps, chans), F32),
            v((heads, wide, wide), F32),
            v((wide, chans), F32),
            v((rows, chans), F32),
            v((taps, rows, chans), F32),
            v((wide, chans), BF16),
            v((wide, states), BF16),
            v((wide, states), BF16),
            v((wide, chans), F32),
            v((wide, chans), F32),
            v((nz, share, 128), BF16),
            v((nz, share, 128), BF16),
            v((nz, 1, chans), F32),
            v((1, chans), F32),
            v((nz, share, 128), F32),
            v((nz, 1, 128), F32),
            v((share + 8, 128), F32),
            v((ny - 1, share + 8, 128), F32),
            v((nz, share, 128), BF16),
            v((nz, share, 128), BF16),
            v((wide, chans), F32),
            v((rows, chans), BF16),
            v((parts, nx, 2, rows // parts, cols), BF16),
            v((parts, nx, rows // parts, cols), BF16),
            v((parts, others, rows // parts, cols), BF16),
            v((parts, others, rows // parts, cols), BF16),
            dma((12,)),
            dma((2, reach + 1)), dma((2, reach + 1)),
            dma((2, reach + 1)), dma((2, reach + 1)),
            dma((nz, ny)), dma((nz, ny)),
            dma((2, reach + 1)), dma((2, reach + 1)),
            dma((2, reach + 1)), dma((2, reach + 1)),
            dma((3, ny)), dma((3, ny)),
            dma((2,)), dma((2,)),
            dma((2,)), dma((2,)),
            dma((nz,)), dma((nz,)),
            dma((nz,)), dma((nz,)),
            dma((ny - 1,)), dma((ny - 1,)),
            dma((nz,)), dma((nz,)),
            dma((parts,)), dma((parts,)),
            dma((parts, others)), dma((parts, others)),
        ]
        hbm = pl.BlockSpec(memory_space=pl.ANY)
        return pl.pallas_call(
            functools.partial(kernel, ny, nz, nx, parts),
            out_shape=jax.ShapeDtypeStruct((rows, cols), BF16),
            in_specs=[pl.BlockSpec(memory_space=pltpu.SMEM)] + [hbm] * 8,
            out_specs=pl.BlockSpec(memory_space=pltpu.VMEM),
            scratch_shapes=scratch,
            compiler_params=pltpu.CompilerParams(
                collective_id=0, has_side_effects=True, vmem_limit_bytes=60 * 2**20
            ),
            name="mixer",
        )(lens, frames, xw, zw, bcw, logd, gain.reshape(1, chans), convw, outw.T)

    in_specs = (
        P("tm", None), P("tm", "head"), P("tm", "head"), P("tm", None), P("head", "tm"),
        P("head"), P(None, "head"), P("head", "tm"), P(),
    )
    return jax.shard_map(
        local, mesh=mesh, in_specs=in_specs, out_specs=P("tm", "head"), check_vma=False
    )
```

```python
import functools

import jax
import jax.numpy as jnp
from jax import lax
from jax.experimental import pallas as pl
from jax.experimental.pallas import tpu as pltpu
from jax.sharding import PartitionSpec as P

NY = 4
EDGE = 16
MESH = pl.DeviceIdType.MESH
HIGHEST = lax.Precision.HIGHEST
F32 = jnp.float32
BF16 = jnp.bfloat16
PS = 64


def nt(a, b, **kw):
    return lax.dot_general(a, b, (((1,), (1,)), ((), ())), preferred_element_type=F32, **kw)


def tn(a, b, **kw):
    return lax.dot_general(a, b, (((0,), (0,)), ((), ())), preferred_element_type=F32, **kw)


def nn(a, b, **kw):
    return jnp.dot(a, b, preferred_element_type=F32, **kw)


def iota(shape, dim):
    return lax.broadcasted_iota(jnp.int32, shape, dim)


def kernel(
    ny, nz, nx, parts,
    lens_in, frames_in, xw, zw, bcw, logd_in, gain_in, convw_in, outw, out,
    lens, w, frames, logd, gain, convw, mix, growth, tail, wm, xs, bs, cs, inner, zs,
    local, got, keeps, keep_own, pref, ckeep, tot, tots, back, entry, ext, act,
    part, pair, red, redin,
    s_loc, s_a1, r_a1, s_a2, r_a2, s_ay, r_ay, s_b, r_b, s_by, r_by,
    s_f, r_f, s_l, r_l, s_k, r_k, s_s, r_s, s_t, r_t, s_p, r_p, s_c, r_c, s_x, r_x,
):
    me, hd = lax.axis_index("tm"), lax.axis_index("head")
    y, z = lax.div(me, nz), lax.rem(me, nz)
    x, core = lax.div(hd, 2), lax.rem(hd, 2)
    tms = ny * nz
    rows, width = frames_in.shape
    depth, chans = xw.shape
    wide = rows + 2 * EDGE
    heads = chans // PS
    states = bcw.shape[1] // 2
    taps = convw_in.shape[0]
    half = (taps - 1) // 2
    reach = max(nz // 4, 1)
    hop = max(nz // 8, 1)
    stages = nz // 2 // hop
    base = me * rows
    first = base - EDGE

    def at(yy, zz):
        return {"tm": yy * nz + zz}

    def turn(a, d, n):
        return lax.rem(a + d + n, n)

    pending = []

    def send(src, dst, ssem, rsem, dev):
        copy = pltpu.make_async_remote_copy(
            src_ref=src, dst_ref=dst, send_sem=ssem, recv_sem=rsem,
            device_id=dev, device_id_type=MESH,
        )
        copy.start()
        pending.append(copy)

    done = [0]

    def drain(upto):
        while done[0] < upto:
            pending[done[0]].wait_send()
            done[0] += 1

    def recv(dst, rsem):
        pltpu.make_async_copy(dst, dst, rsem).wait()

    barrier = pltpu.get_barrier_semaphore()
    greet = [at(y, turn(z, s * k, nz)) for k in range(reach, 0, -1) for s in (1, -1)]
    greet += [at(turn(y, d, ny), z) for d in range(1, ny)]
    greet += [{"tm": turn(me, 1, tms)}, {"tm": turn(me, -1, tms)}]
    greet += [{"head": 2 * turn(x, d, nx) + core} for d in range(1, nx)]
    greet += [{"head": 2 * x + 1 - core}]
    for dev in greet:
        pl.semaphore_signal(barrier, inc=1, device_id=dev, device_id_type=MESH)

    tiles = [(xw, 0), (xw, 128), (bcw, 0), (bcw, 128), (zw, 0), (zw, 128), (outw, 0), (outw, 128)]
    own = [
        pltpu.make_async_copy(src.at[:, lo : lo + 128], w.at[y, z, i], s_loc.at[i])
        for i, (src, lo) in enumerate(tiles)
    ]
    own.append(pltpu.make_async_copy(logd_in, logd.at[1], s_loc.at[8]))
    own.append(pltpu.make_async_copy(frames_in, frames.at[EDGE : EDGE + rows], s_loc.at[9]))
    own.append(pltpu.make_async_copy(gain_in, gain, s_loc.at[10]))
    own.append(pltpu.make_async_copy(convw_in, convw, s_loc.at[11]))
    own.append(pltpu.make_async_copy(lens_in, lens, s_loc.at[12]))
    for copy in own:
        copy.start()
    for copy in own:
        copy.wait()
    pl.semaphore_wait(barrier, len(greet))

    crit, rest = slice(0, 3), slice(3, 8)

    def stage_1(cut, ssem, rsem, reach):
        ref = w.at[y, z, cut]
        for k in range(reach, 0, -1):
            for way, s in ((0, 1), (1, -1)):
                send(ref, ref, ssem.at[way, k], rsem.at[way, k], at(y, turn(z, s * k, nz)))

    def stage_2(cut, ssem, rsem, way, reach):
        s = 1 - 2 * way
        ref = w.at[y, turn(z, -s * reach, nz), cut]
        for j in range(nz // 2 - reach - way, 0, -1):
            send(ref, ref, ssem.at[way, j], rsem.at[way, j], at(y, turn(z, s * j, nz)))

    def cross(off):
        zz = turn(z, -off, nz)
        ref = w.at[y, zz, crit]
        for d in range(1, ny):
            send(ref, ref, s_ay.at[off % nz, d], r_ay.at[off % nz, d], at(turn(y, d, ny), z))

    def rest_ref(way, dist):
        return w.at[y, turn(z, dist if way else -dist, nz), rest]

    def rest_stage(s):
        src = (s - 1) * hop
        for j in range(hop, 0, -1):
            for way in (0, 1):
                dist = src + j
                if dist < nz // 2 or way == 0:
                    ref = rest_ref(way, src)
                    send(ref, ref, s_b.at[way, dist], r_b.at[way, dist],
                         at(y, turn(z, -j if way else j, nz)))

    def rest_cross(off):
        ref = w.at[y, turn(z, -off, nz), rest]
        for d in range(1, ny):
            send(ref, ref, s_by.at[off % nz, d], r_by.at[off % nz, d], at(turn(y, d, ny), z))

    def rest_step(s):
        if s > stages:
            return
        for j in range(hop, 0, -1):
            dist = (s - 1) * hop + j
            for way in (0, 1):
                if dist < nz // 2 or way == 0:
                    recv(rest_ref(way, dist), r_b.at[way, dist])
            if j == hop and s < stages:
                rest_stage(s + 1)
            for way in (0, 1):
                if dist < nz // 2 or way == 0:
                    rest_cross(-dist if way else dist)

    def got_1(cut, rsem, way, k):
        recv(w.at[y, turn(z, k if way else -k, nz), cut], rsem.at[way, k])

    def got_2(cut, rsem, way, j, reach):
        far = reach + j
        recv(w.at[y, turn(z, far if way else -far, nz), cut], rsem.at[way, j])

    stage_1(crit, s_a1, r_a1, reach)
    cross(0)
    for i, d in enumerate((1, -1)):
        send(logd.at[1], logd.at[1 - d], s_l.at[i], r_l.at[i], {"tm": turn(me, d, tms)})
    send(frames.at[rows : rows + EDGE], frames.at[0:EDGE],
         s_f.at[0], r_f.at[0], {"tm": turn(me, 1, tms)})
    send(frames.at[EDGE : 2 * EDGE], frames.at[rows + EDGE : wide],
         s_f.at[1], r_f.at[1], {"tm": turn(me, -1, tms)})

    ends = []
    total = jnp.int32(0)
    for r in range(lens.shape[0]):
        total = total + lens[r]
        ends.append(total)

    def starts(pos):
        start = jnp.zeros(pos.shape, jnp.int32)
        for e in ends:
            start = jnp.where(pos >= e, e, start)
        return start

    pos = first + iota((wide, 1), 0)
    start = starts(pos)
    vals = {}

    def piece_cumul():
        i, j = iota((wide, rows), 0), iota((wide, rows), 1)
        cols = (
            (j >= rows - EDGE) & (j - (rows - EDGE) <= i),
            j + EDGE <= i,
            (j < EDGE) & (j + EDGE + rows <= i),
        )
        cum, line = 0.0, 0.0
        for p, col in enumerate(cols):
            ones = col.astype(F32)
            lines = logd[p]
            spread = jnp.concatenate(
                [jnp.broadcast_to(lines[h : h + 1, :], (PS, rows)) for h in range(heads)], axis=0
            )
            cum = cum + nt(ones, spread, precision=HIGHEST)
            line = line + nt(lines, ones, precision=HIGHEST)
        vals["cum"], vals["line"] = cum, line
        last = cum[rows - 1 : rows, :]
        last_start = start[rows - 1 : rows, :]
        growth[...] = jnp.where(start < first, jnp.exp(cum), 0.0)
        tail[...] = jnp.where(pos[0:rows] >= last_start, jnp.exp(last - cum[0:rows]), 0.0)
        keep_own[...] = jnp.where(last_start < first, jnp.exp(last), 0.0)

    def piece_mix(h):
        i, j = iota((wide, wide), 0), iota((wide, wide), 1)
        joined = (i >= j) & (first + j >= start)
        diff = vals["cum"][:, h * PS : h * PS + 1] - vals["line"][h : h + 1, :]
        mix[h] = jnp.exp(jnp.where(joined, diff, -1e30))

    def piece_taps(k_lo, k_hi):
        lanes = 128
        here = pos[EDGE : EDGE + rows]
        stop = jnp.full(here.shape, ends[-1], jnp.int32)
        for e in reversed(ends):
            stop = jnp.where(here < e, e, stop)
        before = jnp.broadcast_to(start[EDGE : EDGE + rows] - here, (rows, lanes))
        after = jnp.broadcast_to(stop - here, (rows, lanes))
        for k in range(k_lo, k_hi):
            ok = (k - half >= before) if k <= half else (k - half < after)
            for lo in range(0, chans, lanes):
                wm[k, :, lo : lo + lanes] = jnp.where(ok, convw[k : k + 1, lo : lo + lanes], 0.0)

    for way in (0, 1):
        got_1(crit, r_a1, way, reach)
        stage_2(crit, s_a2, r_a2, way, reach)
        cross(reach if way == 0 else -reach)
    rest_stage(1)
    for k in range(reach - 1, 0, -1):
        for way in (0, 1):
            got_1(crit, r_a1, way, k)
            cross(k if way == 0 else -k)
    recv(logd.at[0], r_l.at[0])
    recv(logd.at[2], r_l.at[1])
    piece_cumul()
    for j in range(1, nz // 2 - reach + 1):
        for way in (0, 1):
            if j <= nz // 2 - reach - way:
                got_2(crit, r_a2, way, j, reach)
                cross(reach + j if way == 0 else -(reach + j))
    rest_cross(0)
    rest_step(1)
    keeps[z] = keep_own[...]
    for d in range(1, nz):
        send(keep_own, keeps.at[z], s_k.at[d], r_k.at[d], at(y, turn(z, d, nz)))
    for h in range(heads):
        piece_mix(h)
    recv(frames.at[0:EDGE], r_f.at[0])
    recv(frames.at[rows + EDGE : wide], r_f.at[1])
    for off in range(nz):
        for d in range(1, ny):
            recv(w.at[turn(y, -d, ny), turn(z, -off, nz), crit], r_ay.at[off, d])

    def weight(lo, count):
        return jnp.concatenate(
            [w[:, :, lo + i].reshape(width, 128) for i in range(count)], axis=1
        )

    bs[...] = nn(frames[...], weight(2, 1)).astype(BF16)
    xb = nn(frames[...], weight(0, 2)).astype(BF16)
    xs[...] = xb
    weighted = (xb[0:rows].astype(F32) * tail[...]).astype(BF16)
    state = tn(bs[0:rows], weighted).astype(BF16)
    share = local.shape[1]
    each = nz * 128 // chans
    for lo in range(chans // 128):
        local[lo * each : (lo + 1) * each] = state[:, lo * 128 : lo * 128 + 128].reshape(
            each, share, 128
        )
    mark = len(pending)
    for d in range(1, nz):
        zz = turn(z, d, nz)
        send(local.at[zz], got.at[z], s_s.at[d], r_s.at[d], at(y, zz))
    got[z] = local[z]

    rest_step(2)
    for k in range(0, taps, 4):
        piece_taps(k, min(k + 4, taps))
    rest_step(3)

    for d in range(1, nz):
        recv(keeps.at[turn(z, -d, nz)], r_k.at[d])
    drain(mark)

    for d in range(1, nz):
        zz = turn(z, -d, nz)
        recv(got.at[zz], r_s.at[d])
    carry = jnp.zeros((share, 128), F32)
    decay = jnp.ones((1, 128), F32)
    for zz in range(nz):
        pref[zz] = carry
        ckeep[zz] = decay
        line = keeps[zz]
        keep = line[:, 0:128]
        for lo in range(1, chans // 128):
            keep = jnp.where(lax.div(z, each) == lo, line[:, lo * 128 : lo * 128 + 128], keep)
        carry = carry * keep + got[zz].astype(F32)
        decay = decay * keep
    tot[0:share] = carry
    tot[share : share + 8] = jnp.broadcast_to(decay, (8, 128))
    for d in range(1, ny):
        send(tot, tots.at[d - 1], s_t.at[d - 1], r_t.at[d - 1], at(turn(y, d, ny), z))
    rest_step(4)
    for d in range(1, ny):
        recv(tots.at[d - 1], r_t.at[d - 1])
    come = jnp.zeros((share, 128), F32)
    for d in range(ny - 1, 0, -1):
        new = come * tots[d - 1, share : share + 1] + tots[d - 1, 0:share]
        come = jnp.where(y >= d, new, 0.0)
    for zz in range(nz):
        back[zz] = (pref[zz] + ckeep[zz] * come).astype(BF16)
    mark = len(pending)
    for d in range(1, nz):
        zz = turn(z, d, nz)
        send(back.at[zz], entry.at[z], s_p.at[d], r_p.at[d], at(y, zz))
    entry[z] = back[z]

    for off in range(nz):
        for d in range(1, ny):
            recv(w.at[turn(y, -d, ny), turn(z, -off, nz), rest], r_by.at[off, d])
    cs[...] = nn(frames[...], weight(3, 1)).astype(BF16)
    scores = nt(cs[...], bs[...])
    lane_head = lax.div(iota((wide, chans), 1), PS)
    acc = jnp.zeros((wide, chans), F32)
    for h in range(heads):
        only = jnp.where(lane_head == h, xs[...].astype(F32), 0.0).astype(BF16)
        acc = acc + nn((mix[h] * scores).astype(BF16), only)
    inner[...] = acc
    zr = nn(frames[...], weight(4, 2)).astype(BF16).astype(F32)
    zs[...] = zr * jax.nn.sigmoid(zr) * gain[...]
    same = lax.div(iota((chans, chans), 0), PS) == lax.div(iota((chans, chans), 1), PS)
    block = jnp.where(same, 1.0 / PS, 0.0).astype(BF16)
    drain(mark)

    for d in range(1, nz):
        recv(entry.at[turn(z, -d, nz)], r_p.at[d])
    come_in = jnp.concatenate(
        [entry[lo * each : (lo + 1) * each].reshape(states, 128) for lo in range(chans // 128)],
        axis=1,
    )
    ssd = inner[...] + nn(cs[...], come_in) * growth[...]
    mean = nn((ssd * ssd).astype(BF16), block)
    g = (ssd * lax.rsqrt(mean + 1e-05) * zs[...]).astype(BF16)
    ext[...] = g.astype(F32)

    cols = width // (2 * nx)
    span = rows // parts
    per = cols // depth

    def conv(lo, hi):
        acc = jnp.zeros((hi - lo, chans), F32)
        for k in range(taps):
            off = EDGE - half + k
            acc = acc + wm[k, lo:hi, :] * ext[lo + off : hi + off, :]
        act[lo:hi] = (acc * jax.nn.sigmoid(acc)).astype(BF16)

    ow = weight(6, 2)
    for p in range(parts):
        for lo in range(p * span, (p + 1) * span, 32):
            conv(lo, lo + 32)
        rows_p = act[p * span : (p + 1) * span]
        for j in range(2 * nx):
            part[p, j // 2, j % 2] = nt(rows_p, ow[j * cols : (j + 1) * cols]).astype(BF16)
        send(part.at[p, :, 1 - core], pair.at[p], s_c.at[p], r_c.at[p], {"head": 2 * x + 1 - core})
    for p in range(parts):
        recv(pair.at[p], r_c.at[p])
        for d in range(nx - 1, 0, -1):
            xx = turn(x, d, nx)
            red[p, d - 1] = (part[p, xx, core].astype(F32) + pair[p, xx].astype(F32)).astype(BF16)
            send(red.at[p, d - 1], redin.at[p, d - 1], s_x.at[p, d - 1], r_x.at[p, d - 1],
                 {"head": 2 * xx + core})
    for p in range(parts):
        res = part[p, x, core].astype(F32) + pair[p, x].astype(F32)
        for d in range(1, nx):
            recv(redin.at[p, d - 1], r_x.at[p, d - 1])
            res = res + redin[p, d - 1].astype(F32)
        out[p * span : (p + 1) * span] = res.astype(BF16)
    drain(len(pending))


def solution(mesh):
    tms, groups = mesh.shape["tm"], mesh.shape["head"]
    ny, nz, nx = NY, tms // NY, groups // 2

    def local(frames, xw, zw, bcw, logd, gain, convw, outw, lens):
        rows, width = frames.shape
        depth, chans = xw.shape
        states = bcw.shape[1] // 2
        heads = logd.shape[0]
        taps = convw.shape[0]
        share = states * chans // (nz * 128)
        cols = width // groups
        wide = rows + 2 * EDGE
        parts = 2
        dma = pltpu.SemaphoreType.DMA
        v = pltpu.VMEM
        others = max(nx - 1, 1)
        scratch = [
            pltpu.SMEM(lens.shape, jnp.int32),
            v((ny, nz, 8, depth, 128), BF16),
            v((wide, width), BF16),
            v((3, heads, rows), F32),
            v((1, chans), F32),
            v((taps, chans), F32),
            v((heads, wide, wide), F32),
            v((wide, chans), F32),
            v((rows, chans), F32),
            v((taps, rows, chans), F32),
            v((wide, chans), BF16),
            v((wide, states), BF16),
            v((wide, states), BF16),
            v((wide, chans), F32),
            v((wide, chans), F32),
            v((nz, share, 128), BF16),
            v((nz, share, 128), BF16),
            v((nz, 1, chans), F32),
            v((1, chans), F32),
            v((nz, share, 128), F32),
            v((nz, 1, 128), F32),
            v((share + 8, 128), F32),
            v((ny - 1, share + 8, 128), F32),
            v((nz, share, 128), BF16),
            v((nz, share, 128), BF16),
            v((wide, chans), F32),
            v((rows, chans), BF16),
            v((parts, nx, 2, rows // parts, cols), BF16),
            v((parts, nx, rows // parts, cols), BF16),
            v((parts, others, rows // parts, cols), BF16),
            v((parts, others, rows // parts, cols), BF16),
            dma((13,)),
            dma((2, nz // 2 + 1)), dma((2, nz // 2 + 1)),
            dma((2, nz // 2 + 1)), dma((2, nz // 2 + 1)),
            dma((nz, ny)), dma((nz, ny)),
            dma((2, nz // 2 + 1)), dma((2, nz // 2 + 1)),
            dma((nz, ny)), dma((nz, ny)),
            dma((2,)), dma((2,)),
            dma((2,)), dma((2,)),
            dma((nz,)), dma((nz,)),
            dma((nz,)), dma((nz,)),
            dma((ny - 1,)), dma((ny - 1,)),
            dma((nz,)), dma((nz,)),
            dma((parts,)), dma((parts,)),
            dma((parts, others)), dma((parts, others)),
        ]
        hbm = pl.BlockSpec(memory_space=pl.ANY)
        return pl.pallas_call(
            functools.partial(kernel, ny, nz, nx, parts),
            out_shape=jax.ShapeDtypeStruct((rows, cols), BF16),
            in_specs=[hbm] * 9,
            out_specs=pl.BlockSpec(memory_space=pltpu.VMEM),
            scratch_shapes=scratch,
            compiler_params=pltpu.CompilerParams(
                collective_id=0, has_side_effects=True, vmem_limit_bytes=60 * 2**20
            ),
            name="mixer",
        )(lens, frames, xw, zw, bcw, logd, gain.reshape(1, chans), convw, outw.T)

    in_specs = (
        P("tm", None), P("tm", "head"), P("tm", "head"), P("tm", None), P("head", "tm"),
        P("head"), P(None, "head"), P("head", "tm"), P(),
    )
    return jax.shard_map(
        local, mesh=mesh, in_specs=in_specs, out_specs=P("tm", "head"), check_vma=False
    )
```

```python
import functools

import jax
import jax.numpy as jnp
from jax import lax
from jax.experimental import pallas as pl
from jax.experimental.pallas import tpu as pltpu
from jax.sharding import PartitionSpec as P

NY = 4
EDGE = 16
MESH = pl.DeviceIdType.MESH
HIGHEST = lax.Precision.HIGHEST
F32 = jnp.float32
BF16 = jnp.bfloat16
PS = 64


def nt(a, b, **kw):
    return lax.dot_general(a, b, (((1,), (1,)), ((), ())), preferred_element_type=F32, **kw)


def tn(a, b, **kw):
    return lax.dot_general(a, b, (((0,), (0,)), ((), ())), preferred_element_type=F32, **kw)


def nn(a, b, **kw):
    return jnp.dot(a, b, preferred_element_type=F32, **kw)


def iota(shape, dim):
    return lax.broadcasted_iota(jnp.int32, shape, dim)


def kernel(
    ny, nz, nx, parts,
    lens_in, frames_in, xw, zw, bcw, logd_in, gain_in, convw_in, outw, out,
    lens, w, frames, logd, gain, convw, mix, growth, tail, wm, xs, bs, cs, inner, zs,
    local, got, keeps, keep_own, pref, ckeep, tot, tots, back, entry, ext, act,
    part, pair, red, redin,
    s_loc, s_a1, r_a1, s_a2, r_a2, s_ay, r_ay, s_b, r_b, s_by, r_by,
    s_f, r_f, s_l, r_l, s_k, r_k, s_s, r_s, s_t, r_t, s_p, r_p, s_c, r_c, s_x, r_x,
):
    me, hd = lax.axis_index("tm"), lax.axis_index("head")
    y, z = lax.div(me, nz), lax.rem(me, nz)
    x, core = lax.div(hd, 2), lax.rem(hd, 2)
    tms = ny * nz
    rows, width = frames_in.shape
    depth, chans = xw.shape
    wide = rows + 2 * EDGE
    heads = chans // PS
    states = bcw.shape[1] // 2
    taps = convw_in.shape[0]
    half = (taps - 1) // 2
    reach = max(nz // 4, 1)
    hop = max(nz // 8, 1)
    stages = nz // 2 // hop
    base = me * rows
    first = base - EDGE

    def at(yy, zz):
        return {"tm": yy * nz + zz}

    def turn(a, d, n):
        return lax.rem(a + d + n, n)

    pending = []

    def send(src, dst, ssem, rsem, dev):
        copy = pltpu.make_async_remote_copy(
            src_ref=src, dst_ref=dst, send_sem=ssem, recv_sem=rsem,
            device_id=dev, device_id_type=MESH,
        )
        copy.start()
        pending.append(copy)

    done = [0]

    def drain(upto):
        while done[0] < upto:
            pending[done[0]].wait_send()
            done[0] += 1

    def recv(dst, rsem):
        pltpu.make_async_copy(dst, dst, rsem).wait()

    barrier = pltpu.get_barrier_semaphore()
    greet = [at(y, turn(z, s * k, nz)) for k in range(reach, 0, -1) for s in (1, -1)]
    greet += [at(turn(y, d, ny), z) for d in range(1, ny)]
    greet += [{"tm": turn(me, 1, tms)}, {"tm": turn(me, -1, tms)}]
    greet += [{"head": 2 * turn(x, d, nx) + core} for d in range(1, nx)]
    greet += [{"head": 2 * x + 1 - core}]
    for dev in greet:
        pl.semaphore_signal(barrier, inc=1, device_id=dev, device_id_type=MESH)

    tiles = [(xw, 0), (xw, 128), (bcw, 0), (bcw, 128), (zw, 0), (zw, 128), (outw, 0), (outw, 128)]
    own = [
        pltpu.make_async_copy(src.at[:, lo : lo + 128], w.at[y, z, i], s_loc.at[i])
        for i, (src, lo) in enumerate(tiles)
    ]
    own.append(pltpu.make_async_copy(logd_in, logd.at[1], s_loc.at[8]))
    own.append(pltpu.make_async_copy(frames_in, frames.at[EDGE : EDGE + rows], s_loc.at[9]))
    own.append(pltpu.make_async_copy(gain_in, gain, s_loc.at[10]))
    own.append(pltpu.make_async_copy(convw_in, convw, s_loc.at[11]))
    own.append(pltpu.make_async_copy(lens_in, lens, s_loc.at[12]))
    for copy in own:
        copy.start()
    for copy in own:
        copy.wait()
    pl.semaphore_wait(barrier, len(greet))

    crit, rest = slice(0, 3), slice(3, 8)

    def stage_1(cut, ssem, rsem, reach):
        ref = w.at[y, z, cut]
        for k in range(reach, 0, -1):
            for way, s in ((0, 1), (1, -1)):
                send(ref, ref, ssem.at[way, k], rsem.at[way, k], at(y, turn(z, s * k, nz)))

    def stage_2(cut, ssem, rsem, way, reach):
        s = 1 - 2 * way
        ref = w.at[y, turn(z, -s * reach, nz), cut]
        for j in range(nz // 2 - reach - way, 0, -1):
            send(ref, ref, ssem.at[way, j], rsem.at[way, j], at(y, turn(z, s * j, nz)))

    def cross(off):
        zz = turn(z, -off, nz)
        ref = w.at[y, zz, crit]
        for d in range(1, ny):
            send(ref, ref, s_ay.at[off % nz, d], r_ay.at[off % nz, d], at(turn(y, d, ny), z))

    def rest_ref(way, dist):
        return w.at[y, turn(z, dist if way else -dist, nz), rest]

    def rest_stage(s):
        src = (s - 1) * hop
        for j in range(hop, 0, -1):
            for way in (0, 1):
                dist = src + j
                if dist < nz // 2 or way == 0:
                    ref = rest_ref(way, src)
                    send(ref, ref, s_b.at[way, dist], r_b.at[way, dist],
                         at(y, turn(z, -j if way else j, nz)))

    def rest_cross(off):
        ref = w.at[y, turn(z, -off, nz), rest]
        for d in range(1, ny):
            send(ref, ref, s_by.at[off % nz, d], r_by.at[off % nz, d], at(turn(y, d, ny), z))

    def rest_step(s):
        if s > stages:
            return
        for j in range(hop, 0, -1):
            dist = (s - 1) * hop + j
            for way in (0, 1):
                if dist < nz // 2 or way == 0:
                    recv(rest_ref(way, dist), r_b.at[way, dist])
            if j == hop and s < stages:
                rest_stage(s + 1)
            for way in (0, 1):
                if dist < nz // 2 or way == 0:
                    rest_cross(-dist if way else dist)

    def got_1(cut, rsem, way, k):
        recv(w.at[y, turn(z, k if way else -k, nz), cut], rsem.at[way, k])

    def got_2(cut, rsem, way, j, reach):
        far = reach + j
        recv(w.at[y, turn(z, far if way else -far, nz), cut], rsem.at[way, j])

    stage_1(crit, s_a1, r_a1, reach)
    cross(0)
    for i, d in enumerate((1, -1)):
        send(logd.at[1], logd.at[1 - d], s_l.at[i], r_l.at[i], {"tm": turn(me, d, tms)})
    send(frames.at[rows : rows + EDGE], frames.at[0:EDGE],
         s_f.at[0], r_f.at[0], {"tm": turn(me, 1, tms)})
    send(frames.at[EDGE : 2 * EDGE], frames.at[rows + EDGE : wide],
         s_f.at[1], r_f.at[1], {"tm": turn(me, -1, tms)})

    ends = []
    total = jnp.int32(0)
    for r in range(lens.shape[0]):
        total = total + lens[r]
        ends.append(total)

    def starts(pos):
        start = jnp.zeros(pos.shape, jnp.int32)
        for e in ends:
            start = jnp.where(pos >= e, e, start)
        return start

    pos = first + iota((wide, 1), 0)
    start = starts(pos)
    vals = {}

    def piece_cumul():
        i, j = iota((wide, rows), 0), iota((wide, rows), 1)
        cols = (
            (j >= rows - EDGE) & (j - (rows - EDGE) <= i),
            j + EDGE <= i,
            (j < EDGE) & (j + EDGE + rows <= i),
        )
        cum, line = 0.0, 0.0
        for p, col in enumerate(cols):
            ones = col.astype(F32)
            lines = logd[p]
            spread = jnp.concatenate(
                [jnp.broadcast_to(lines[h : h + 1, :], (PS, rows)) for h in range(heads)], axis=0
            )
            cum = cum + nt(ones, spread, precision=HIGHEST)
            line = line + nt(lines, ones, precision=HIGHEST)
        vals["cum"], vals["line"] = cum, line
        last = cum[rows - 1 : rows, :]
        last_start = start[rows - 1 : rows, :]
        growth[...] = jnp.where(start < first, jnp.exp(cum), 0.0)
        tail[...] = jnp.where(pos[0:rows] >= last_start, jnp.exp(last - cum[0:rows]), 0.0)
        keep_own[...] = jnp.where(last_start < first, jnp.exp(last), 0.0)

    def piece_mix(h):
        i, j = iota((wide, wide), 0), iota((wide, wide), 1)
        joined = (i >= j) & (first + j >= start)
        diff = vals["cum"][:, h * PS : h * PS + 1] - vals["line"][h : h + 1, :]
        mix[h] = jnp.exp(jnp.where(joined, diff, -1e30))

    def piece_taps(k_lo, k_hi):
        lanes = 128
        here = pos[EDGE : EDGE + rows]
        stop = jnp.full(here.shape, ends[-1], jnp.int32)
        for e in reversed(ends):
            stop = jnp.where(here < e, e, stop)
        before = jnp.broadcast_to(start[EDGE : EDGE + rows] - here, (rows, lanes))
        after = jnp.broadcast_to(stop - here, (rows, lanes))
        for k in range(k_lo, k_hi):
            ok = (k - half >= before) if k <= half else (k - half < after)
            for lo in range(0, chans, lanes):
                wm[k, :, lo : lo + lanes] = jnp.where(ok, convw[k : k + 1, lo : lo + lanes], 0.0)

    for way in (0, 1):
        got_1(crit, r_a1, way, reach)
        stage_2(crit, s_a2, r_a2, way, reach)
        cross(reach if way == 0 else -reach)
    rest_stage(1)
    for k in range(reach - 1, 0, -1):
        for way in (0, 1):
            got_1(crit, r_a1, way, k)
            cross(k if way == 0 else -k)
    recv(logd.at[0], r_l.at[0])
    recv(logd.at[2], r_l.at[1])
    piece_cumul()
    for j in range(1, nz // 2 - reach + 1):
        for way in (0, 1):
            if j <= nz // 2 - reach - way:
                got_2(crit, r_a2, way, j, reach)
                cross(reach + j if way == 0 else -(reach + j))
    rest_cross(0)
    rest_step(1)
    keeps[z] = keep_own[...]
    for d in range(1, nz):
        send(keep_own, keeps.at[z], s_k.at[d], r_k.at[d], at(y, turn(z, d, nz)))
    for h in range(heads):
        piece_mix(h)
    recv(frames.at[0:EDGE], r_f.at[0])
    recv(frames.at[rows + EDGE : wide], r_f.at[1])
    for off in range(nz):
        for d in range(1, ny):
            recv(w.at[turn(y, -d, ny), turn(z, -off, nz), crit], r_ay.at[off, d])

    def weight(lo, count):
        return jnp.concatenate(
            [w[:, :, lo + i].reshape(width, 128) for i in range(count)], axis=1
        )

    bs[...] = nn(frames[...], weight(2, 1)).astype(BF16)
    xb = nn(frames[...], weight(0, 2)).astype(BF16)
    xs[...] = xb
    weighted = (xb[0:rows].astype(F32) * tail[...]).astype(BF16)
    state = tn(bs[0:rows], weighted).astype(BF16)
    share = local.shape[1]
    each = nz * 128 // chans
    for lo in range(chans // 128):
        local[lo * each : (lo + 1) * each] = state[:, lo * 128 : lo * 128 + 128].reshape(
            each, share, 128
        )
    mark = len(pending)
    for d in range(1, nz):
        zz = turn(z, d, nz)
        send(local.at[zz], got.at[z], s_s.at[d], r_s.at[d], at(y, zz))
    got[z] = local[z]

    rest_step(2)
    for k in range(0, taps, 4):
        piece_taps(k, min(k + 4, taps))
    rest_step(3)

    for d in range(1, nz):
        recv(keeps.at[turn(z, -d, nz)], r_k.at[d])
    drain(mark)

    for d in range(1, nz):
        zz = turn(z, -d, nz)
        recv(got.at[zz], r_s.at[d])
    carry = jnp.zeros((share, 128), F32)
    decay = jnp.ones((1, 128), F32)
    for zz in range(nz):
        pref[zz] = carry
        ckeep[zz] = decay
        line = keeps[zz]
        keep = line[:, 0:128]
        for lo in range(1, chans // 128):
            keep = jnp.where(lax.div(z, each) == lo, line[:, lo * 128 : lo * 128 + 128], keep)
        carry = carry * keep + got[zz].astype(F32)
        decay = decay * keep
    tot[0:share] = carry
    tot[share : share + 8] = jnp.broadcast_to(decay, (8, 128))
    for d in range(1, ny):
        send(tot, tots.at[d - 1], s_t.at[d - 1], r_t.at[d - 1], at(turn(y, d, ny), z))
    rest_step(4)
    for d in range(1, ny):
        recv(tots.at[d - 1], r_t.at[d - 1])
    come = jnp.zeros((share, 128), F32)
    for d in range(ny - 1, 0, -1):
        new = come * tots[d - 1, share : share + 1] + tots[d - 1, 0:share]
        come = jnp.where(y >= d, new, 0.0)
    for zz in range(nz):
        back[zz] = (pref[zz] + ckeep[zz] * come).astype(BF16)
    mark = len(pending)
    for d in range(1, nz):
        zz = turn(z, d, nz)
        send(back.at[zz], entry.at[z], s_p.at[d], r_p.at[d], at(y, zz))
    entry[z] = back[z]

    for off in range(nz):
        for d in range(1, ny):
            recv(w.at[turn(y, -d, ny), turn(z, -off, nz), rest], r_by.at[off, d])
    cs[...] = nn(frames[...], weight(3, 1)).astype(BF16)
    scores = nt(cs[...], bs[...])
    lane_head = lax.div(iota((wide, chans), 1), PS)
    acc = jnp.zeros((wide, chans), F32)
    for h in range(heads):
        only = jnp.where(lane_head == h, xs[...].astype(F32), 0.0).astype(BF16)
        acc = acc + nn((mix[h] * scores).astype(BF16), only)
    inner[...] = acc
    zr = nn(frames[...], weight(4, 2)).astype(BF16).astype(F32)
    zs[...] = zr * jax.nn.sigmoid(zr) * gain[...]
    same = lax.div(iota((chans, chans), 0), PS) == lax.div(iota((chans, chans), 1), PS)
    block = jnp.where(same, 1.0 / PS, 0.0).astype(BF16)
    drain(mark)

    for d in range(1, nz):
        recv(entry.at[turn(z, -d, nz)], r_p.at[d])
    come_in = jnp.concatenate(
        [entry[lo * each : (lo + 1) * each].reshape(states, 128) for lo in range(chans // 128)],
        axis=1,
    )
    ssd = inner[...] + nn(cs[...], come_in) * growth[...]
    mean = nn((ssd * ssd).astype(BF16), block)
    g = (ssd * lax.rsqrt(mean + 1e-05) * zs[...]).astype(BF16)
    ext[...] = g.astype(F32)

    cols = width // (2 * nx)
    span = rows // parts
    per = cols // depth

    def conv(lo, hi):
        acc = jnp.zeros((hi - lo, chans), F32)
        for k in range(taps):
            off = EDGE - half + k
            acc = acc + wm[k, lo:hi, :] * ext[lo + off : hi + off, :]
        act[lo:hi] = (acc * jax.nn.sigmoid(acc)).astype(BF16)

    ow = weight(6, 2)
    for p in range(parts):
        for lo in range(p * span, (p + 1) * span, 32):
            conv(lo, lo + 32)
        rows_p = act[p * span : (p + 1) * span]
        for j in range(2 * nx):
            part[p, j // 2, j % 2] = nt(rows_p, ow[j * cols : (j + 1) * cols]).astype(BF16)
        send(part.at[p, :, 1 - core], pair.at[p], s_c.at[p], r_c.at[p], {"head": 2 * x + 1 - core})
    for p in range(parts):
        recv(pair.at[p], r_c.at[p])
        for d in range(nx - 1, 0, -1):
            xx = turn(x, d, nx)
            red[p, d - 1] = (part[p, xx, core].astype(F32) + pair[p, xx].astype(F32)).astype(BF16)
            send(red.at[p, d - 1], redin.at[p, d - 1], s_x.at[p, d - 1], r_x.at[p, d - 1],
                 {"head": 2 * xx + core})
    for p in range(parts):
        res = part[p, x, core].astype(F32) + pair[p, x].astype(F32)
        for d in range(1, nx):
            recv(redin.at[p, d - 1], r_x.at[p, d - 1])
            res = res + redin[p, d - 1].astype(F32)
        out[p * span : (p + 1) * span] = res.astype(BF16)
    drain(len(pending))


def solution(mesh):
    tms, groups = mesh.shape["tm"], mesh.shape["head"]
    ny, nz, nx = NY, tms // NY, groups // 2

    def local(frames, xw, zw, bcw, logd, gain, convw, outw, lens):
        rows, width = frames.shape
        depth, chans = xw.shape
        states = bcw.shape[1] // 2
        heads = logd.shape[0]
        taps = convw.shape[0]
        share = states * chans // (nz * 128)
        cols = width // groups
        wide = rows + 2 * EDGE
        parts = 4
        dma = pltpu.SemaphoreType.DMA
        v = pltpu.VMEM
        others = max(nx - 1, 1)
        scratch = [
            pltpu.SMEM(lens.shape, jnp.int32),
            v((ny, nz, 8, depth, 128), BF16),
            v((wide, width), BF16),
            v((3, heads, rows), F32),
            v((1, chans), F32),
            v((taps, chans), F32),
            v((heads, wide, wide), F32),
            v((wide, chans), F32),
            v((rows, chans), F32),
            v((taps, rows, chans), F32),
            v((wide, chans), BF16),
            v((wide, states), BF16),
            v((wide, states), BF16),
            v((wide, chans), F32),
            v((wide, chans), F32),
            v((nz, share, 128), BF16),
            v((nz, share, 128), BF16),
            v((nz, 1, chans), F32),
            v((1, chans), F32),
            v((nz, share, 128), F32),
            v((nz, 1, 128), F32),
            v((share + 8, 128), F32),
            v((ny - 1, share + 8, 128), F32),
            v((nz, share, 128), BF16),
            v((nz, share, 128), BF16),
            v((wide, chans), F32),
            v((rows, chans), BF16),
            v((parts, nx, 2, rows // parts, cols), BF16),
            v((parts, nx, rows // parts, cols), BF16),
            v((parts, others, rows // parts, cols), BF16),
            v((parts, others, rows // parts, cols), BF16),
            dma((13,)),
            dma((2, nz // 2 + 1)), dma((2, nz // 2 + 1)),
            dma((2, nz // 2 + 1)), dma((2, nz // 2 + 1)),
            dma((nz, ny)), dma((nz, ny)),
            dma((2, nz // 2 + 1)), dma((2, nz // 2 + 1)),
            dma((nz, ny)), dma((nz, ny)),
            dma((2,)), dma((2,)),
            dma((2,)), dma((2,)),
            dma((nz,)), dma((nz,)),
            dma((nz,)), dma((nz,)),
            dma((ny - 1,)), dma((ny - 1,)),
            dma((nz,)), dma((nz,)),
            dma((parts,)), dma((parts,)),
            dma((parts, others)), dma((parts, others)),
        ]
        hbm = pl.BlockSpec(memory_space=pltpu.HBM)
        return pl.pallas_call(
            functools.partial(kernel, ny, nz, nx, parts),
            out_shape=jax.ShapeDtypeStruct((rows, cols), BF16),
            in_specs=[hbm] * 9,
            out_specs=pl.BlockSpec(memory_space=pltpu.VMEM),
            scratch_shapes=scratch,
            compiler_params=pltpu.CompilerParams(
                collective_id=0, has_side_effects=True, vmem_limit_bytes=28 * 2**20
            ),
            name="mixer",
        )(*[
            pltpu.with_memory_space_constraint(v, pltpu.HBM)
            for v in (lens, frames, xw, zw, bcw, logd, gain.reshape(1, chans), convw, outw.T)
        ])

    in_specs = (
        P("tm", None), P("tm", "head"), P("tm", "head"), P("tm", None), P("head", "tm"),
        P("head"), P(None, "head"), P("head", "tm"), P(),
    )
    return jax.shard_map(
        local, mesh=mesh, in_specs=in_specs, out_specs=P("tm", "head"), check_vma=False
    )
```

```python
import functools

import jax
import jax.numpy as jnp
from jax import lax
from jax.experimental import pallas as pl
from jax.experimental.pallas import tpu as pltpu
from jax.sharding import PartitionSpec as P

NY = 4
EDGE = 16
MESH = pl.DeviceIdType.MESH
HIGHEST = lax.Precision.HIGHEST
F32 = jnp.float32
BF16 = jnp.bfloat16
PS = 64


def nt(a, b, **kw):
    return lax.dot_general(a, b, (((1,), (1,)), ((), ())), preferred_element_type=F32, **kw)


def tn(a, b, **kw):
    return lax.dot_general(a, b, (((0,), (0,)), ((), ())), preferred_element_type=F32, **kw)


def nn(a, b, **kw):
    return jnp.dot(a, b, preferred_element_type=F32, **kw)


def iota(shape, dim):
    return lax.broadcasted_iota(jnp.int32, shape, dim)


def kernel(
    ny, nz, nx, parts,
    lens_in, frames_in, xw, zw, bcw, logd_in, gain_in, convw_in, outw, out,
    lens, w, frames, logd, gain, convw, mix, growth, tail, wm, xs, bs, cs, inner, zs,
    local, got, keeps, keep_own, pref, ckeep, tot, tots, back, entry, ext, act,
    part, pair, red, redin,
    s_loc, s_a1, r_a1, s_a2, r_a2, s_ay, r_ay, s_b, r_b, s_by, r_by,
    s_f, r_f, s_l, r_l, s_k, r_k, s_s, r_s, s_t, r_t, s_p, r_p, s_c, r_c, s_x, r_x,
):
    me, hd = lax.axis_index("tm"), lax.axis_index("head")
    y, z = lax.div(me, nz), lax.rem(me, nz)
    x, core = lax.div(hd, 2), lax.rem(hd, 2)
    tms = ny * nz
    rows, width = frames_in.shape
    depth, chans = xw.shape
    wide = rows + 2 * EDGE
    heads = chans // PS
    states = bcw.shape[1] // 2
    taps = convw_in.shape[0]
    half = (taps - 1) // 2
    reach = max(nz // 4, 1)
    hop = max(nz // 8, 1)
    stages = nz // 2 // hop
    base = me * rows
    first = base - EDGE

    def at(yy, zz):
        return {"tm": yy * nz + zz}

    def turn(a, d, n):
        return lax.rem(a + d + n, n)

    def ring(n):
        return sorted(range(1, n), key=lambda d: (-min(d, n - d), d))

    pending = []

    def send(src, dst, ssem, rsem, dev):
        copy = pltpu.make_async_remote_copy(
            src_ref=src, dst_ref=dst, send_sem=ssem, recv_sem=rsem,
            device_id=dev, device_id_type=MESH,
        )
        copy.start()
        pending.append(copy)

    done = [0]

    def drain(upto):
        while done[0] < upto:
            pending[done[0]].wait_send()
            done[0] += 1

    def recv(dst, rsem):
        pltpu.make_async_copy(dst, dst, rsem).wait()

    barrier = pltpu.get_barrier_semaphore()
    greet = [at(y, turn(z, s * k, nz)) for k in range(reach, 0, -1) for s in (1, -1)]
    greet += [at(turn(y, d, ny), z) for d in range(1, ny)]
    greet += [{"tm": turn(me, 1, tms)}, {"tm": turn(me, -1, tms)}]
    greet += [{"head": 2 * turn(x, d, nx) + core} for d in range(1, nx)]
    greet += [{"head": 2 * x + 1 - core}]
    for dev in greet:
        pl.semaphore_signal(barrier, inc=1, device_id=dev, device_id_type=MESH)

    tiles = [(xw, 0), (xw, 128), (bcw, 0), (bcw, 128), (zw, 0), (zw, 128), (outw, 0), (outw, 128)]
    own = [
        pltpu.make_async_copy(src.at[:, lo : lo + 128], w.at[y, z, i], s_loc.at[i])
        for i, (src, lo) in enumerate(tiles)
    ]
    own.append(pltpu.make_async_copy(logd_in, logd.at[1], s_loc.at[8]))
    own.append(pltpu.make_async_copy(frames_in, frames.at[EDGE : EDGE + rows], s_loc.at[9]))
    own.append(pltpu.make_async_copy(gain_in, gain, s_loc.at[10]))
    own.append(pltpu.make_async_copy(convw_in, convw, s_loc.at[11]))
    own.append(pltpu.make_async_copy(lens_in, lens, s_loc.at[12]))
    for copy in own:
        copy.start()
    for copy in own[0:3]:
        copy.wait()
    pl.semaphore_wait(barrier, len(greet))

    crit, rest = slice(0, 3), slice(3, 8)

    def stage_1(cut, ssem, rsem, reach):
        ref = w.at[y, z, cut]
        for k in range(reach, 0, -1):
            for way, s in ((0, 1), (1, -1)):
                send(ref, ref, ssem.at[way, k], rsem.at[way, k], at(y, turn(z, s * k, nz)))

    def stage_2(cut, ssem, rsem, way, reach):
        s = 1 - 2 * way
        ref = w.at[y, turn(z, -s * reach, nz), cut]
        for j in range(nz // 2 - reach - way, 0, -1):
            send(ref, ref, ssem.at[way, j], rsem.at[way, j], at(y, turn(z, s * j, nz)))

    def cross(off):
        zz = turn(z, -off, nz)
        ref = w.at[y, zz, crit]
        for d in ring(ny):
            send(ref, ref, s_ay.at[off % nz, d], r_ay.at[off % nz, d], at(turn(y, d, ny), z))

    def rest_ref(way, dist):
        return w.at[y, turn(z, dist if way else -dist, nz), rest]

    def rest_stage(s):
        src = (s - 1) * hop
        for j in range(hop, 0, -1):
            for way in (0, 1):
                dist = src + j
                if dist < nz // 2 or way == 0:
                    ref = rest_ref(way, src)
                    send(ref, ref, s_b.at[way, dist], r_b.at[way, dist],
                         at(y, turn(z, -j if way else j, nz)))

    def rest_cross(off):
        ref = w.at[y, turn(z, -off, nz), rest]
        for d in ring(ny):
            send(ref, ref, s_by.at[off % nz, d], r_by.at[off % nz, d], at(turn(y, d, ny), z))

    def rest_step(s):
        if s > stages:
            return
        for j in range(hop, 0, -1):
            dist = (s - 1) * hop + j
            for way in (0, 1):
                if dist < nz // 2 or way == 0:
                    recv(rest_ref(way, dist), r_b.at[way, dist])
            if j == hop and s < stages:
                rest_stage(s + 1)
            for way in (0, 1):
                if dist < nz // 2 or way == 0:
                    rest_cross(-dist if way else dist)

    def got_1(cut, rsem, way, k):
        recv(w.at[y, turn(z, k if way else -k, nz), cut], rsem.at[way, k])

    def got_2(cut, rsem, way, j, reach):
        far = reach + j
        recv(w.at[y, turn(z, far if way else -far, nz), cut], rsem.at[way, j])

    stage_1(crit, s_a1, r_a1, reach)
    cross(0)
    for copy in own[3:]:
        copy.wait()
    for i, d in enumerate((1, -1)):
        send(logd.at[1], logd.at[1 - d], s_l.at[i], r_l.at[i], {"tm": turn(me, d, tms)})
    send(frames.at[rows : rows + EDGE], frames.at[0:EDGE],
         s_f.at[0], r_f.at[0], {"tm": turn(me, 1, tms)})
    send(frames.at[EDGE : 2 * EDGE], frames.at[rows + EDGE : wide],
         s_f.at[1], r_f.at[1], {"tm": turn(me, -1, tms)})

    ends = []
    total = jnp.int32(0)
    for r in range(lens.shape[0]):
        total = total + lens[r]
        ends.append(total)

    def starts(pos):
        start = jnp.zeros(pos.shape, jnp.int32)
        for e in ends:
            start = jnp.where(pos >= e, e, start)
        return start

    pos = first + iota((wide, 1), 0)
    start = starts(pos)
    vals = {}

    def piece_cumul():
        i, j = iota((wide, rows), 0), iota((wide, rows), 1)
        cols = (
            (j >= rows - EDGE) & (j - (rows - EDGE) <= i),
            j + EDGE <= i,
            (j < EDGE) & (j + EDGE + rows <= i),
        )
        cum, line = 0.0, 0.0
        for p, col in enumerate(cols):
            ones = col.astype(F32)
            lines = logd[p]
            spread = jnp.concatenate(
                [jnp.broadcast_to(lines[h : h + 1, :], (PS, rows)) for h in range(heads)], axis=0
            )
            cum = cum + nt(ones, spread, precision=HIGHEST)
            line = line + nt(lines, ones, precision=HIGHEST)
        vals["cum"], vals["line"] = cum, line
        last = cum[rows - 1 : rows, :]
        last_start = start[rows - 1 : rows, :]
        growth[...] = jnp.where(start < first, jnp.exp(cum), 0.0)
        tail[...] = jnp.where(pos[0:rows] >= last_start, jnp.exp(last - cum[0:rows]), 0.0)
        keep_own[...] = jnp.where(last_start < first, jnp.exp(last), 0.0)

    def piece_mix(h):
        i, j = iota((wide, wide), 0), iota((wide, wide), 1)
        joined = (i >= j) & (first + j >= start)
        diff = vals["cum"][:, h * PS : h * PS + 1] - vals["line"][h : h + 1, :]
        mix[h] = jnp.exp(jnp.where(joined, diff, -1e30))

    def piece_taps(k_lo, k_hi):
        lanes = 128
        here = pos[EDGE : EDGE + rows]
        stop = jnp.full(here.shape, ends[-1], jnp.int32)
        for e in reversed(ends):
            stop = jnp.where(here < e, e, stop)
        before = jnp.broadcast_to(start[EDGE : EDGE + rows] - here, (rows, lanes))
        after = jnp.broadcast_to(stop - here, (rows, lanes))
        for k in range(k_lo, k_hi):
            ok = (k - half >= before) if k <= half else (k - half < after)
            for lo in range(0, chans, lanes):
                wm[k, :, lo : lo + lanes] = jnp.where(ok, convw[k : k + 1, lo : lo + lanes], 0.0)

    for way in (0, 1):
        got_1(crit, r_a1, way, reach)
        stage_2(crit, s_a2, r_a2, way, reach)
        cross(reach if way == 0 else -reach)
    rest_stage(1)
    for k in range(reach - 1, 0, -1):
        for way in (0, 1):
            got_1(crit, r_a1, way, k)
            cross(k if way == 0 else -k)
    recv(logd.at[0], r_l.at[0])
    recv(logd.at[2], r_l.at[1])
    piece_cumul()
    for j in range(1, nz // 2 - reach + 1):
        for way in (0, 1):
            if j <= nz // 2 - reach - way:
                got_2(crit, r_a2, way, j, reach)
                cross(reach + j if way == 0 else -(reach + j))
    rest_cross(0)
    rest_step(1)
    keeps[z] = keep_own[...]
    for d in ring(nz):
        send(keep_own, keeps.at[z], s_k.at[d], r_k.at[d], at(y, turn(z, d, nz)))
    for h in range(heads):
        piece_mix(h)
    recv(frames.at[0:EDGE], r_f.at[0])
    recv(frames.at[rows + EDGE : wide], r_f.at[1])
    for off in range(nz):
        for d in range(1, ny):
            recv(w.at[turn(y, -d, ny), turn(z, -off, nz), crit], r_ay.at[off, d])

    def weight(lo, count):
        return jnp.concatenate(
            [w[:, :, lo + i].reshape(width, 128) for i in range(count)], axis=1
        )

    bs[...] = nn(frames[...], weight(2, 1)).astype(BF16)
    xb = nn(frames[...], weight(0, 2)).astype(BF16)
    xs[...] = xb
    weighted = (xb[0:rows].astype(F32) * tail[...]).astype(BF16)
    state = tn(bs[0:rows], weighted).astype(BF16)
    share = local.shape[1]
    each = nz * 128 // chans
    for lo in range(chans // 128):
        local[lo * each : (lo + 1) * each] = state[:, lo * 128 : lo * 128 + 128].reshape(
            each, share, 128
        )
    mark = len(pending)
    for d in ring(nz):
        zz = turn(z, d, nz)
        send(local.at[zz], got.at[z], s_s.at[d], r_s.at[d], at(y, zz))
    got[z] = local[z]

    rest_step(2)
    for k in range(0, taps, 4):
        piece_taps(k, min(k + 4, taps))
    rest_step(3)

    for d in range(1, nz):
        recv(keeps.at[turn(z, -d, nz)], r_k.at[d])
    drain(mark)

    for d in range(1, nz):
        zz = turn(z, -d, nz)
        recv(got.at[zz], r_s.at[d])
    carry = jnp.zeros((share, 128), F32)
    decay = jnp.ones((1, 128), F32)
    for zz in range(nz):
        pref[zz] = carry
        ckeep[zz] = decay
        line = keeps[zz]
        keep = line[:, 0:128]
        for lo in range(1, chans // 128):
            keep = jnp.where(lax.div(z, each) == lo, line[:, lo * 128 : lo * 128 + 128], keep)
        carry = carry * keep + got[zz].astype(F32)
        decay = decay * keep
    tot[0:share] = carry
    tot[share : share + 8] = jnp.broadcast_to(decay, (8, 128))
    for d in ring(ny):
        send(tot, tots.at[d - 1], s_t.at[d - 1], r_t.at[d - 1], at(turn(y, d, ny), z))
    rest_step(4)
    for d in range(1, ny):
        recv(tots.at[d - 1], r_t.at[d - 1])
    come = jnp.zeros((share, 128), F32)
    for d in range(ny - 1, 0, -1):
        new = come * tots[d - 1, share : share + 1] + tots[d - 1, 0:share]
        come = jnp.where(y >= d, new, 0.0)
    for zz in range(nz):
        back[zz] = (pref[zz] + ckeep[zz] * come).astype(BF16)
    mark = len(pending)
    for d in ring(nz):
        zz = turn(z, d, nz)
        send(back.at[zz], entry.at[z], s_p.at[d], r_p.at[d], at(y, zz))
    entry[z] = back[z]

    for off in range(nz):
        for d in range(1, ny):
            recv(w.at[turn(y, -d, ny), turn(z, -off, nz), rest], r_by.at[off, d])
    cs[...] = nn(frames[...], weight(3, 1)).astype(BF16)
    scores = nt(cs[...], bs[...])
    lane_head = lax.div(iota((wide, chans), 1), PS)
    acc = jnp.zeros((wide, chans), F32)
    for h in range(heads):
        only = jnp.where(lane_head == h, xs[...].astype(F32), 0.0).astype(BF16)
        acc = acc + nn((mix[h] * scores).astype(BF16), only)
    inner[...] = acc
    zr = nn(frames[...], weight(4, 2)).astype(BF16).astype(F32)
    zs[...] = zr * jax.nn.sigmoid(zr) * gain[...]
    same = lax.div(iota((chans, chans), 0), PS) == lax.div(iota((chans, chans), 1), PS)
    block = jnp.where(same, 1.0 / PS, 0.0).astype(BF16)
    drain(mark)

    for d in range(1, nz):
        recv(entry.at[turn(z, -d, nz)], r_p.at[d])
    come_in = jnp.concatenate(
        [entry[lo * each : (lo + 1) * each].reshape(states, 128) for lo in range(chans // 128)],
        axis=1,
    )
    ssd = inner[...] + nn(cs[...], come_in) * growth[...]
    mean = nn((ssd * ssd).astype(BF16), block)
    g = (ssd * lax.rsqrt(mean + 1e-05) * zs[...]).astype(BF16)
    ext[...] = g.astype(F32)

    cols = width // (2 * nx)
    span = rows // parts
    per = cols // depth

    def conv(lo, hi):
        acc = jnp.zeros((hi - lo, chans), F32)
        for k in range(taps):
            off = EDGE - half + k
            acc = acc + wm[k, lo:hi, :] * ext[lo + off : hi + off, :]
        act[lo:hi] = (acc * jax.nn.sigmoid(acc)).astype(BF16)

    ow = weight(6, 2)
    for p in range(parts):
        for lo in range(p * span, (p + 1) * span, 32):
            conv(lo, lo + 32)
        rows_p = act[p * span : (p + 1) * span]
        for j in range(2 * nx):
            part[p, j // 2, j % 2] = nt(rows_p, ow[j * cols : (j + 1) * cols]).astype(BF16)
        send(part.at[p, :, 1 - core], pair.at[p], s_c.at[p], r_c.at[p], {"head": 2 * x + 1 - core})
    for p in range(parts):
        recv(pair.at[p], r_c.at[p])
        for d in ring(nx):
            xx = turn(x, d, nx)
            red[p, d - 1] = (part[p, xx, core].astype(F32) + pair[p, xx].astype(F32)).astype(BF16)
            send(red.at[p, d - 1], redin.at[p, d - 1], s_x.at[p, d - 1], r_x.at[p, d - 1],
                 {"head": 2 * xx + core})
    for p in range(parts):
        res = part[p, x, core].astype(F32) + pair[p, x].astype(F32)
        for d in range(1, nx):
            recv(redin.at[p, d - 1], r_x.at[p, d - 1])
            res = res + redin[p, d - 1].astype(F32)
        out[p * span : (p + 1) * span] = res.astype(BF16)
    drain(len(pending))


def solution(mesh):
    tms, groups = mesh.shape["tm"], mesh.shape["head"]
    ny, nz, nx = NY, tms // NY, groups // 2

    def local(frames, xw, zw, bcw, logd, gain, convw, outw, lens):
        rows, width = frames.shape
        depth, chans = xw.shape
        states = bcw.shape[1] // 2
        heads = logd.shape[0]
        taps = convw.shape[0]
        share = states * chans // (nz * 128)
        cols = width // groups
        wide = rows + 2 * EDGE
        parts = 4
        dma = pltpu.SemaphoreType.DMA
        v = pltpu.VMEM
        others = max(nx - 1, 1)
        scratch = [
            pltpu.SMEM(lens.shape, jnp.int32),
            v((ny, nz, 8, depth, 128), BF16),
            v((wide, width), BF16),
            v((3, heads, rows), F32),
            v((1, chans), F32),
            v((taps, chans), F32),
            v((heads, wide, wide), F32),
            v((wide, chans), F32),
            v((rows, chans), F32),
            v((taps, rows, chans), F32),
            v((wide, chans), BF16),
            v((wide, states), BF16),
            v((wide, states), BF16),
            v((wide, chans), F32),
            v((wide, chans), F32),
            v((nz, share, 128), BF16),
            v((nz, share, 128), BF16),
            v((nz, 1, chans), F32),
            v((1, chans), F32),
            v((nz, share, 128), F32),
            v((nz, 1, 128), F32),
            v((share + 8, 128), F32),
            v((ny - 1, share + 8, 128), F32),
            v((nz, share, 128), BF16),
            v((nz, share, 128), BF16),
            v((wide, chans), F32),
            v((rows, chans), BF16),
            v((parts, nx, 2, rows // parts, cols), BF16),
            v((parts, nx, rows // parts, cols), BF16),
            v((parts, others, rows // parts, cols), BF16),
            v((parts, others, rows // parts, cols), BF16),
            dma((13,)),
            dma((2, nz // 2 + 1)), dma((2, nz // 2 + 1)),
            dma((2, nz // 2 + 1)), dma((2, nz // 2 + 1)),
            dma((nz, ny)), dma((nz, ny)),
            dma((2, nz // 2 + 1)), dma((2, nz // 2 + 1)),
            dma((nz, ny)), dma((nz, ny)),
            dma((2,)), dma((2,)),
            dma((2,)), dma((2,)),
            dma((nz,)), dma((nz,)),
            dma((nz,)), dma((nz,)),
            dma((ny - 1,)), dma((ny - 1,)),
            dma((nz,)), dma((nz,)),
            dma((parts,)), dma((parts,)),
            dma((parts, others)), dma((parts, others)),
        ]
        hbm = pl.BlockSpec(memory_space=pltpu.HBM)
        return pl.pallas_call(
            functools.partial(kernel, ny, nz, nx, parts),
            out_shape=jax.ShapeDtypeStruct((rows, cols), BF16),
            in_specs=[hbm] * 9,
            out_specs=pl.BlockSpec(memory_space=pltpu.VMEM),
            scratch_shapes=scratch,
            compiler_params=pltpu.CompilerParams(
                collective_id=0, has_side_effects=True, vmem_limit_bytes=28 * 2**20
            ),
            name="mixer",
        )(*[
            pltpu.with_memory_space_constraint(v, pltpu.HBM)
            for v in (lens, frames, xw, zw, bcw, logd, gain.reshape(1, chans), convw, outw.T)
        ])

    in_specs = (
        P("tm", None), P("tm", "head"), P("tm", "head"), P("tm", None), P("head", "tm"),
        P("head"), P(None, "head"), P("head", "tm"), P(),
    )
    return jax.shard_map(
        local, mesh=mesh, in_specs=in_specs, out_specs=P("tm", "head"), check_vma=False
    )
```

```python
import functools

import jax
import jax.numpy as jnp
from jax import lax
from jax.experimental import pallas as pl
from jax.experimental.pallas import tpu as pltpu
from jax.sharding import PartitionSpec as P

NY = 4
EDGE = 16
MESH = pl.DeviceIdType.MESH
HIGHEST = lax.Precision.HIGHEST
F32 = jnp.float32
BF16 = jnp.bfloat16
PS = 64


def nt(a, b, **kw):
    return lax.dot_general(a, b, (((1,), (1,)), ((), ())), preferred_element_type=F32, **kw)


def tn(a, b, **kw):
    return lax.dot_general(a, b, (((0,), (0,)), ((), ())), preferred_element_type=F32, **kw)


def nn(a, b, **kw):
    return jnp.dot(a, b, preferred_element_type=F32, **kw)


def iota(shape, dim):
    return lax.broadcasted_iota(jnp.int32, shape, dim)


def kernel(
    ny, nz, nx, parts,
    lens_in, frames_in, xw, zw, bcw, logd_in, gain_in, convw_in, outw, out,
    lens, w, frames, logd, gain, convw, mix, growth, tail, wm, xs, bs, cs, inner, zs,
    local, got, keeps, keep_own, pref, ckeep, tot, tots, back, entry, ext, act,
    part, pair, red, redin,
    s_loc, s_a1, r_a1, s_a2, r_a2, s_ay, r_ay, s_b, r_b, s_by, r_by,
    s_f, r_f, s_l, r_l, s_k, r_k, s_s, r_s, s_t, r_t, s_p, r_p, s_c, r_c, s_x, r_x,
):
    me, hd = lax.axis_index("tm"), lax.axis_index("head")
    y, z = lax.div(me, nz), lax.rem(me, nz)
    x, core = lax.div(hd, 2), lax.rem(hd, 2)
    tms = ny * nz
    rows, width = frames_in.shape
    depth, chans = xw.shape
    wide = rows + 2 * EDGE
    heads = chans // PS
    states = bcw.shape[1] // 2
    taps = convw_in.shape[0]
    half = (taps - 1) // 2
    reach = max(nz // 4, 1)
    hop = max(nz // 8, 1)
    stages = nz // 2 // hop
    base = me * rows
    first = base - EDGE

    def at(yy, zz):
        return {"tm": yy * nz + zz}

    def turn(a, d, n):
        return lax.rem(a + d + n, n)

    def ring(n):
        return sorted(range(1, n), key=lambda d: (-min(d, n - d), d))

    pending = []

    def send(src, dst, ssem, rsem, dev):
        copy = pltpu.make_async_remote_copy(
            src_ref=src, dst_ref=dst, send_sem=ssem, recv_sem=rsem,
            device_id=dev, device_id_type=MESH,
        )
        copy.start()
        pending.append(copy)

    done = [0]

    def drain(upto):
        while done[0] < upto:
            pending[done[0]].wait_send()
            done[0] += 1

    def recv(dst, rsem):
        pltpu.make_async_copy(dst, dst, rsem).wait()

    barrier = pltpu.get_barrier_semaphore()
    greet = [at(y, turn(z, s * k, nz)) for k in range(reach, 0, -1) for s in (1, -1)]
    greet += [at(turn(y, d, ny), z) for d in range(1, ny)]
    greet += [{"tm": turn(me, 1, tms)}, {"tm": turn(me, -1, tms)}]
    greet += [{"head": 2 * turn(x, d, nx) + core} for d in range(1, nx)]
    greet += [{"head": 2 * x + 1 - core}]
    for dev in greet:
        pl.semaphore_signal(barrier, inc=1, device_id=dev, device_id_type=MESH)

    tiles = [(xw, 0), (xw, 128), (bcw, 0), (bcw, 128), (zw, 0), (zw, 128), (outw, 0), (outw, 128)]
    own = [
        pltpu.make_async_copy(src.at[:, lo : lo + 128], w.at[y, z, i], s_loc.at[i])
        for i, (src, lo) in enumerate(tiles)
    ]
    own.append(pltpu.make_async_copy(logd_in, logd.at[1], s_loc.at[8]))
    own.append(pltpu.make_async_copy(frames_in, frames.at[EDGE : EDGE + rows], s_loc.at[9]))
    own.append(pltpu.make_async_copy(gain_in, gain, s_loc.at[10]))
    own.append(pltpu.make_async_copy(convw_in, convw, s_loc.at[11]))
    own.append(pltpu.make_async_copy(lens_in, lens, s_loc.at[12]))
    for copy in own:
        copy.start()
    for copy in own[0:3]:
        copy.wait()
    pl.semaphore_wait(barrier, len(greet))

    crit, rest = slice(0, 3), slice(3, 8)

    def stage_1(cut, ssem, rsem, reach):
        ref = w.at[y, z, cut]
        for k in range(reach, 0, -1):
            for way, s in ((0, 1), (1, -1)):
                send(ref, ref, ssem.at[way, k], rsem.at[way, k], at(y, turn(z, s * k, nz)))

    def stage_2(cut, ssem, rsem, way, reach):
        s = 1 - 2 * way
        ref = w.at[y, turn(z, -s * reach, nz), cut]
        for j in range(nz // 2 - reach - way, 0, -1):
            send(ref, ref, ssem.at[way, j], rsem.at[way, j], at(y, turn(z, s * j, nz)))

    def cross(off):
        zz = turn(z, -off, nz)
        ref = w.at[y, zz, crit]
        for d in ring(ny):
            send(ref, ref, s_ay.at[off % nz, d], r_ay.at[off % nz, d], at(turn(y, d, ny), z))

    def rest_ref(way, dist):
        return w.at[y, turn(z, dist if way else -dist, nz), rest]

    def rest_stage(s):
        src = (s - 1) * hop
        for j in range(hop, 0, -1):
            for way in (0, 1):
                dist = src + j
                if dist < nz // 2 or way == 0:
                    ref = rest_ref(way, src)
                    send(ref, ref, s_b.at[way, dist], r_b.at[way, dist],
                         at(y, turn(z, -j if way else j, nz)))

    def rest_cross(off):
        ref = w.at[y, turn(z, -off, nz), rest]
        for d in ring(ny):
            send(ref, ref, s_by.at[off % nz, d], r_by.at[off % nz, d], at(turn(y, d, ny), z))

    def rest_step(s):
        if s > stages:
            return
        for j in range(hop, 0, -1):
            dist = (s - 1) * hop + j
            for way in (0, 1):
                if dist < nz // 2 or way == 0:
                    recv(rest_ref(way, dist), r_b.at[way, dist])
            if j == hop and s < stages:
                rest_stage(s + 1)
            for way in (0, 1):
                if dist < nz // 2 or way == 0:
                    rest_cross(-dist if way else dist)

    def got_1(cut, rsem, way, k):
        recv(w.at[y, turn(z, k if way else -k, nz), cut], rsem.at[way, k])

    def got_2(cut, rsem, way, j, reach):
        far = reach + j
        recv(w.at[y, turn(z, far if way else -far, nz), cut], rsem.at[way, j])

    stage_1(crit, s_a1, r_a1, reach)
    cross(0)
    for copy in own[3:]:
        copy.wait()
    for i, d in enumerate((1, -1)):
        send(logd.at[1], logd.at[1 - d], s_l.at[i], r_l.at[i], {"tm": turn(me, d, tms)})
    send(frames.at[rows : rows + EDGE], frames.at[0:EDGE],
         s_f.at[0], r_f.at[0], {"tm": turn(me, 1, tms)})
    send(frames.at[EDGE : 2 * EDGE], frames.at[rows + EDGE : wide],
         s_f.at[1], r_f.at[1], {"tm": turn(me, -1, tms)})
    rest_stage(1)
    rest_cross(0)

    ends = []
    total = jnp.int32(0)
    for r in range(lens.shape[0]):
        total = total + lens[r]
        ends.append(total)

    def starts(pos):
        start = jnp.zeros(pos.shape, jnp.int32)
        for e in ends:
            start = jnp.where(pos >= e, e, start)
        return start

    pos = first + iota((wide, 1), 0)
    start = starts(pos)
    vals = {}

    def piece_cumul():
        i, j = iota((wide, rows), 0), iota((wide, rows), 1)
        cols = (
            (j >= rows - EDGE) & (j - (rows - EDGE) <= i),
            j + EDGE <= i,
            (j < EDGE) & (j + EDGE + rows <= i),
        )
        cum, line = 0.0, 0.0
        for p, col in enumerate(cols):
            ones = col.astype(F32)
            lines = logd[p]
            spread = jnp.concatenate(
                [jnp.broadcast_to(lines[h : h + 1, :], (PS, rows)) for h in range(heads)], axis=0
            )
            cum = cum + nt(ones, spread, precision=HIGHEST)
            line = line + nt(lines, ones, precision=HIGHEST)
        vals["cum"], vals["line"] = cum, line
        last = cum[rows - 1 : rows, :]
        last_start = start[rows - 1 : rows, :]
        growth[...] = jnp.where(start < first, jnp.exp(cum), 0.0)
        tail[...] = jnp.where(pos[0:rows] >= last_start, jnp.exp(last - cum[0:rows]), 0.0)
        keep_own[...] = jnp.where(last_start < first, jnp.exp(last), 0.0)

    def piece_mix(h):
        i, j = iota((wide, wide), 0), iota((wide, wide), 1)
        joined = (i >= j) & (first + j >= start)
        diff = vals["cum"][:, h * PS : h * PS + 1] - vals["line"][h : h + 1, :]
        mix[h] = jnp.exp(jnp.where(joined, diff, -1e30))

    def piece_taps(k_lo, k_hi):
        lanes = 128
        here = pos[EDGE : EDGE + rows]
        stop = jnp.full(here.shape, ends[-1], jnp.int32)
        for e in reversed(ends):
            stop = jnp.where(here < e, e, stop)
        before = jnp.broadcast_to(start[EDGE : EDGE + rows] - here, (rows, lanes))
        after = jnp.broadcast_to(stop - here, (rows, lanes))
        for k in range(k_lo, k_hi):
            ok = (k - half >= before) if k <= half else (k - half < after)
            for lo in range(0, chans, lanes):
                wm[k, :, lo : lo + lanes] = jnp.where(ok, convw[k : k + 1, lo : lo + lanes], 0.0)

    for way in (0, 1):
        got_1(crit, r_a1, way, reach)
        stage_2(crit, s_a2, r_a2, way, reach)
        cross(reach if way == 0 else -reach)
    for k in range(reach - 1, 0, -1):
        for way in (0, 1):
            got_1(crit, r_a1, way, k)
            cross(k if way == 0 else -k)
    recv(logd.at[0], r_l.at[0])
    recv(logd.at[2], r_l.at[1])
    piece_cumul()
    for j in range(1, nz // 2 - reach + 1):
        for way in (0, 1):
            if j <= nz // 2 - reach - way:
                got_2(crit, r_a2, way, j, reach)
                cross(reach + j if way == 0 else -(reach + j))
    rest_step(1)
    keeps[z] = keep_own[...]
    for d in ring(nz):
        send(keep_own, keeps.at[z], s_k.at[d], r_k.at[d], at(y, turn(z, d, nz)))
    for h in range(heads):
        piece_mix(h)
    recv(frames.at[0:EDGE], r_f.at[0])
    recv(frames.at[rows + EDGE : wide], r_f.at[1])
    for off in range(nz):
        for d in range(1, ny):
            recv(w.at[turn(y, -d, ny), turn(z, -off, nz), crit], r_ay.at[off, d])

    def weight(lo, count):
        return jnp.concatenate(
            [w[:, :, lo + i].reshape(width, 128) for i in range(count)], axis=1
        )

    bs[...] = nn(frames[...], weight(2, 1)).astype(BF16)
    xb = nn(frames[...], weight(0, 2)).astype(BF16)
    xs[...] = xb
    weighted = (xb[0:rows].astype(F32) * tail[...]).astype(BF16)
    state = tn(bs[0:rows], weighted).astype(BF16)
    share = local.shape[1]
    each = nz * 128 // chans
    for lo in range(chans // 128):
        local[lo * each : (lo + 1) * each] = state[:, lo * 128 : lo * 128 + 128].reshape(
            each, share, 128
        )
    mark = len(pending)
    for d in ring(nz):
        zz = turn(z, d, nz)
        send(local.at[zz], got.at[z], s_s.at[d], r_s.at[d], at(y, zz))
    got[z] = local[z]

    rest_step(2)
    for k in range(0, taps, 4):
        piece_taps(k, min(k + 4, taps))
    rest_step(3)

    for d in range(1, nz):
        recv(keeps.at[turn(z, -d, nz)], r_k.at[d])
    drain(mark)

    for d in range(1, nz):
        zz = turn(z, -d, nz)
        recv(got.at[zz], r_s.at[d])
    carry = jnp.zeros((share, 128), F32)
    decay = jnp.ones((1, 128), F32)
    for zz in range(nz):
        pref[zz] = carry
        ckeep[zz] = decay
        line = keeps[zz]
        keep = line[:, 0:128]
        for lo in range(1, chans // 128):
            keep = jnp.where(lax.div(z, each) == lo, line[:, lo * 128 : lo * 128 + 128], keep)
        carry = carry * keep + got[zz].astype(F32)
        decay = decay * keep
    tot[0:share] = carry
    tot[share : share + 8] = jnp.broadcast_to(decay, (8, 128))
    for d in ring(ny):
        send(tot, tots.at[d - 1], s_t.at[d - 1], r_t.at[d - 1], at(turn(y, d, ny), z))
    rest_step(4)
    for d in range(1, ny):
        recv(tots.at[d - 1], r_t.at[d - 1])
    come = jnp.zeros((share, 128), F32)
    for d in range(ny - 1, 0, -1):
        new = come * tots[d - 1, share : share + 1] + tots[d - 1, 0:share]
        come = jnp.where(y >= d, new, 0.0)
    for zz in range(nz):
        back[zz] = (pref[zz] + ckeep[zz] * come).astype(BF16)
    mark = len(pending)
    for d in ring(nz):
        zz = turn(z, d, nz)
        send(back.at[zz], entry.at[z], s_p.at[d], r_p.at[d], at(y, zz))
    entry[z] = back[z]

    for off in range(nz):
        for d in range(1, ny):
            recv(w.at[turn(y, -d, ny), turn(z, -off, nz), rest], r_by.at[off, d])
    cs[...] = nn(frames[...], weight(3, 1)).astype(BF16)
    scores = nt(cs[...], bs[...])
    lane_head = lax.div(iota((wide, chans), 1), PS)
    acc = jnp.zeros((wide, chans), F32)
    for h in range(heads):
        only = jnp.where(lane_head == h, xs[...].astype(F32), 0.0).astype(BF16)
        acc = acc + nn((mix[h] * scores).astype(BF16), only)
    inner[...] = acc
    zr = nn(frames[...], weight(4, 2)).astype(BF16).astype(F32)
    zs[...] = zr * jax.nn.sigmoid(zr) * gain[...]
    same = lax.div(iota((chans, chans), 0), PS) == lax.div(iota((chans, chans), 1), PS)
    block = jnp.where(same, 1.0 / PS, 0.0).astype(BF16)
    drain(mark)

    for d in range(1, nz):
        recv(entry.at[turn(z, -d, nz)], r_p.at[d])
    come_in = jnp.concatenate(
        [entry[lo * each : (lo + 1) * each].reshape(states, 128) for lo in range(chans // 128)],
        axis=1,
    )
    ssd = inner[...] + nn(cs[...], come_in) * growth[...]
    mean = nn((ssd * ssd).astype(BF16), block)
    g = (ssd * lax.rsqrt(mean + 1e-05) * zs[...]).astype(BF16)
    ext[...] = g.astype(F32)

    cols = width // (2 * nx)
    span = rows // parts
    per = cols // depth

    def conv(lo, hi):
        acc = jnp.zeros((hi - lo, chans), F32)
        for k in range(taps):
            off = EDGE - half + k
            acc = acc + wm[k, lo:hi, :] * ext[lo + off : hi + off, :]
        act[lo:hi] = (acc * jax.nn.sigmoid(acc)).astype(BF16)

    ow = weight(6, 2)
    for p in range(parts):
        for lo in range(p * span, (p + 1) * span, 32):
            conv(lo, lo + 32)
        rows_p = act[p * span : (p + 1) * span]
        for j in range(2 * nx):
            part[p, j // 2, j % 2] = nt(rows_p, ow[j * cols : (j + 1) * cols]).astype(BF16)
        send(part.at[p, :, 1 - core], pair.at[p], s_c.at[p], r_c.at[p], {"head": 2 * x + 1 - core})
    for p in range(parts):
        recv(pair.at[p], r_c.at[p])
        for d in ring(nx):
            xx = turn(x, d, nx)
            red[p, d - 1] = (part[p, xx, core].astype(F32) + pair[p, xx].astype(F32)).astype(BF16)
            send(red.at[p, d - 1], redin.at[p, d - 1], s_x.at[p, d - 1], r_x.at[p, d - 1],
                 {"head": 2 * xx + core})
    for p in range(parts):
        res = part[p, x, core].astype(F32) + pair[p, x].astype(F32)
        for d in range(1, nx):
            recv(redin.at[p, d - 1], r_x.at[p, d - 1])
            res = res + redin[p, d - 1].astype(F32)
        out[p * span : (p + 1) * span] = res.astype(BF16)
    drain(len(pending))


def solution(mesh):
    tms, groups = mesh.shape["tm"], mesh.shape["head"]
    ny, nz, nx = NY, tms // NY, groups // 2

    def local(frames, xw, zw, bcw, logd, gain, convw, outw, lens):
        rows, width = frames.shape
        depth, chans = xw.shape
        states = bcw.shape[1] // 2
        heads = logd.shape[0]
        taps = convw.shape[0]
        share = states * chans // (nz * 128)
        cols = width // groups
        wide = rows + 2 * EDGE
        parts = 4
        dma = pltpu.SemaphoreType.DMA
        v = pltpu.VMEM
        others = max(nx - 1, 1)
        scratch = [
            pltpu.SMEM(lens.shape, jnp.int32),
            v((ny, nz, 8, depth, 128), BF16),
            v((wide, width), BF16),
            v((3, heads, rows), F32),
            v((1, chans), F32),
            v((taps, chans), F32),
            v((heads, wide, wide), F32),
            v((wide, chans), F32),
            v((rows, chans), F32),
            v((taps, rows, chans), F32),
            v((wide, chans), BF16),
            v((wide, states), BF16),
            v((wide, states), BF16),
            v((wide, chans), F32),
            v((wide, chans), F32),
            v((nz, share, 128), BF16),
            v((nz, share, 128), BF16),
            v((nz, 1, chans), F32),
            v((1, chans), F32),
            v((nz, share, 128), F32),
            v((nz, 1, 128), F32),
            v((share + 8, 128), F32),
            v((ny - 1, share + 8, 128), F32),
            v((nz, share, 128), BF16),
            v((nz, share, 128), BF16),
            v((wide, chans), F32),
            v((rows, chans), BF16),
            v((parts, nx, 2, rows // parts, cols), BF16),
            v((parts, nx, rows // parts, cols), BF16),
            v((parts, others, rows // parts, cols), BF16),
            v((parts, others, rows // parts, cols), BF16),
            dma((13,)),
            dma((2, nz // 2 + 1)), dma((2, nz // 2 + 1)),
            dma((2, nz // 2 + 1)), dma((2, nz // 2 + 1)),
            dma((nz, ny)), dma((nz, ny)),
            dma((2, nz // 2 + 1)), dma((2, nz // 2 + 1)),
            dma((nz, ny)), dma((nz, ny)),
            dma((2,)), dma((2,)),
            dma((2,)), dma((2,)),
            dma((nz,)), dma((nz,)),
            dma((nz,)), dma((nz,)),
            dma((ny - 1,)), dma((ny - 1,)),
            dma((nz,)), dma((nz,)),
            dma((parts,)), dma((parts,)),
            dma((parts, others)), dma((parts, others)),
        ]
        hbm = pl.BlockSpec(memory_space=pltpu.HBM)
        return pl.pallas_call(
            functools.partial(kernel, ny, nz, nx, parts),
            out_shape=jax.ShapeDtypeStruct((rows, cols), BF16),
            in_specs=[hbm] * 9,
            out_specs=pl.BlockSpec(memory_space=pltpu.VMEM),
            scratch_shapes=scratch,
            compiler_params=pltpu.CompilerParams(
                collective_id=0, has_side_effects=True, vmem_limit_bytes=28 * 2**20
            ),
            name="mixer",
        )(*[
            pltpu.with_memory_space_constraint(v, pltpu.HBM)
            for v in (lens, frames, xw, zw, bcw, logd, gain.reshape(1, chans), convw, outw.T)
        ])

    in_specs = (
        P("tm", None), P("tm", "head"), P("tm", "head"), P("tm", None), P("head", "tm"),
        P("head"), P(None, "head"), P("head", "tm"), P(),
    )
    return jax.shard_map(
        local, mesh=mesh, in_specs=in_specs, out_specs=P("tm", "head"), check_vma=False
    )
```

```python
import functools

import jax
import jax.numpy as jnp
from jax import lax
from jax.experimental import pallas as pl
from jax.experimental.pallas import tpu as pltpu
from jax.sharding import PartitionSpec as P

NY = 4
EDGE = 16
MESH = pl.DeviceIdType.MESH
HIGHEST = lax.Precision.HIGHEST
F32 = jnp.float32
BF16 = jnp.bfloat16
PS = 64


def nt(a, b, **kw):
    return lax.dot_general(a, b, (((1,), (1,)), ((), ())), preferred_element_type=F32, **kw)


def tn(a, b, **kw):
    return lax.dot_general(a, b, (((0,), (0,)), ((), ())), preferred_element_type=F32, **kw)


def nn(a, b, **kw):
    return jnp.dot(a, b, preferred_element_type=F32, **kw)


def iota(shape, dim):
    return lax.broadcasted_iota(jnp.int32, shape, dim)


def kernel(
    ny, nz, nx, parts,
    lens_in, frames_in, xw, zw, bcw, logd_in, gain_in, convw_in, outw, out,
    lens, w, frames, logd, gain, convw, mix, growth, tail, wm, xs, bs, cs, inner, zs,
    local, got, keeps, keep_own, pref, ckeep, tot, tots, back, entry, ext, act,
    part, pair, red, redin,
    s_loc, s_a1, r_a1, s_a2, r_a2, s_ay, r_ay, s_b, r_b, s_by, r_by,
    s_f, r_f, s_l, r_l, s_k, r_k, s_s, r_s, s_t, r_t, s_p, r_p, s_c, r_c, s_x, r_x,
):
    me, hd = lax.axis_index("tm"), lax.axis_index("head")
    y, z = lax.div(me, nz), lax.rem(me, nz)
    x, core = lax.div(hd, 2), lax.rem(hd, 2)
    tms = ny * nz
    rows, width = frames_in.shape
    depth, chans = xw.shape
    wide = rows + 2 * EDGE
    heads = chans // PS
    states = bcw.shape[1] // 2
    taps = convw_in.shape[0]
    half = (taps - 1) // 2
    reach = max(nz // 4, 1)
    hop = max(nz // 8, 1)
    stages = nz // 2 // hop
    base = me * rows
    first = base - EDGE

    def at(yy, zz):
        return {"tm": yy * nz + zz}

    def turn(a, d, n):
        return lax.rem(a + d + n, n)

    def ring(n):
        return sorted(range(1, n), key=lambda d: (-min(d, n - d), d))

    pending = []

    def send(src, dst, ssem, rsem, dev):
        copy = pltpu.make_async_remote_copy(
            src_ref=src, dst_ref=dst, send_sem=ssem, recv_sem=rsem,
            device_id=dev, device_id_type=MESH,
        )
        copy.start()
        pending.append(copy)

    done = [0]

    def drain(upto):
        while done[0] < upto:
            pending[done[0]].wait_send()
            done[0] += 1

    def recv(dst, rsem):
        pltpu.make_async_copy(dst, dst, rsem).wait()

    barrier = pltpu.get_barrier_semaphore()
    greet = [at(y, turn(z, s * k, nz)) for k in range(reach, 0, -1) for s in (1, -1)]
    greet += [at(turn(y, d, ny), z) for d in range(1, ny)]
    greet += [{"tm": turn(me, 1, tms)}, {"tm": turn(me, -1, tms)}]
    greet += [{"head": 2 * turn(x, d, nx) + core} for d in range(1, nx)]
    greet += [{"head": 2 * x + 1 - core}]
    for dev in greet:
        pl.semaphore_signal(barrier, inc=1, device_id=dev, device_id_type=MESH)

    tiles = [(xw, 0), (xw, 128), (bcw, 0), (bcw, 128), (zw, 0), (zw, 128), (outw, 0), (outw, 128)]
    own = [
        pltpu.make_async_copy(src.at[:, lo : lo + 128], w.at[y, z, i], s_loc.at[i])
        for i, (src, lo) in enumerate(tiles)
    ]
    own.append(pltpu.make_async_copy(logd_in, logd.at[1], s_loc.at[8]))
    own.append(pltpu.make_async_copy(frames_in, frames.at[EDGE : EDGE + rows], s_loc.at[9]))
    own.append(pltpu.make_async_copy(gain_in, gain, s_loc.at[10]))
    own.append(pltpu.make_async_copy(convw_in, convw, s_loc.at[11]))
    own.append(pltpu.make_async_copy(lens_in, lens, s_loc.at[12]))
    for copy in own:
        copy.start()
    for copy in own[0:3]:
        copy.wait()
    pl.semaphore_wait(barrier, len(greet))

    crit, rest = slice(0, 3), slice(3, 8)

    def stage_1(cut, ssem, rsem, reach):
        ref = w.at[y, z, cut]
        for k in range(reach, 0, -1):
            for way, s in ((0, 1), (1, -1)):
                send(ref, ref, ssem.at[way, k], rsem.at[way, k], at(y, turn(z, s * k, nz)))

    def stage_2(cut, ssem, rsem, way, reach):
        s = 1 - 2 * way
        ref = w.at[y, turn(z, -s * reach, nz), cut]
        for j in range(nz // 2 - reach - way, 0, -1):
            send(ref, ref, ssem.at[way, j], rsem.at[way, j], at(y, turn(z, s * j, nz)))

    def cross(off):
        zz = turn(z, -off, nz)
        ref = w.at[y, zz, crit]
        for d in ring(ny):
            send(ref, ref, s_ay.at[off % nz, d], r_ay.at[off % nz, d], at(turn(y, d, ny), z))

    def rest_ref(way, dist):
        return w.at[y, turn(z, dist if way else -dist, nz), rest]

    def rest_stage(s):
        src = (s - 1) * hop
        for j in range(hop, 0, -1):
            for way in (0, 1):
                dist = src + j
                if dist < nz // 2 or way == 0:
                    ref = rest_ref(way, src)
                    send(ref, ref, s_b.at[way, dist], r_b.at[way, dist],
                         at(y, turn(z, -j if way else j, nz)))

    def rest_cross(off):
        ref = w.at[y, turn(z, -off, nz), rest]
        for d in ring(ny):
            send(ref, ref, s_by.at[off % nz, d], r_by.at[off % nz, d], at(turn(y, d, ny), z))

    def rest_step(s):
        if s > stages:
            return
        for j in range(hop, 0, -1):
            dist = (s - 1) * hop + j
            for way in (0, 1):
                if dist < nz // 2 or way == 0:
                    recv(rest_ref(way, dist), r_b.at[way, dist])
            if j == hop and s < stages:
                rest_stage(s + 1)
            for way in (0, 1):
                if dist < nz // 2 or way == 0:
                    rest_cross(-dist if way else dist)

    def got_1(cut, rsem, way, k):
        recv(w.at[y, turn(z, k if way else -k, nz), cut], rsem.at[way, k])

    def got_2(cut, rsem, way, j, reach):
        far = reach + j
        recv(w.at[y, turn(z, far if way else -far, nz), cut], rsem.at[way, j])

    stage_1(crit, s_a1, r_a1, reach)
    cross(0)
    for copy in own[3:]:
        copy.wait()
    for i, d in enumerate((1, -1)):
        send(logd.at[1], logd.at[1 - d], s_l.at[i], r_l.at[i], {"tm": turn(me, d, tms)})
    send(frames.at[rows : rows + EDGE], frames.at[0:EDGE],
         s_f.at[0], r_f.at[0], {"tm": turn(me, 1, tms)})
    send(frames.at[EDGE : 2 * EDGE], frames.at[rows + EDGE : wide],
         s_f.at[1], r_f.at[1], {"tm": turn(me, -1, tms)})

    ends = []
    total = jnp.int32(0)
    for r in range(lens.shape[0]):
        total = total + lens[r]
        ends.append(total)

    def starts(pos):
        start = jnp.zeros(pos.shape, jnp.int32)
        for e in ends:
            start = jnp.where(pos >= e, e, start)
        return start

    pos = first + iota((wide, 1), 0)
    start = starts(pos)
    vals = {}

    def piece_cumul():
        i, j = iota((wide, rows), 0), iota((wide, rows), 1)
        cols = (
            (j >= rows - EDGE) & (j - (rows - EDGE) <= i),
            j + EDGE <= i,
            (j < EDGE) & (j + EDGE + rows <= i),
        )
        cum, line = 0.0, 0.0
        for p, col in enumerate(cols):
            ones = col.astype(F32)
            lines = logd[p]
            spread = jnp.concatenate(
                [jnp.broadcast_to(lines[h : h + 1, :], (PS, rows)) for h in range(heads)], axis=0
            )
            cum = cum + nt(ones, spread, precision=HIGHEST)
            line = line + nt(lines, ones, precision=HIGHEST)
        vals["cum"], vals["line"] = cum, line
        last = cum[rows - 1 : rows, :]
        last_start = start[rows - 1 : rows, :]
        growth[...] = jnp.where(start < first, jnp.exp(cum), 0.0)
        tail[...] = jnp.where(pos[0:rows] >= last_start, jnp.exp(last - cum[0:rows]), 0.0)
        keep_own[...] = jnp.where(last_start < first, jnp.exp(last), 0.0)

    def piece_mix(h):
        i, j = iota((wide, wide), 0), iota((wide, wide), 1)
        joined = (i >= j) & (first + j >= start)
        diff = vals["cum"][:, h * PS : h * PS + 1] - vals["line"][h : h + 1, :]
        mix[h] = jnp.exp(jnp.where(joined, diff, -1e30))

    def piece_taps(k_lo, k_hi):
        lanes = 128
        here = pos[EDGE : EDGE + rows]
        stop = jnp.full(here.shape, ends[-1], jnp.int32)
        for e in reversed(ends):
            stop = jnp.where(here < e, e, stop)
        before = jnp.broadcast_to(start[EDGE : EDGE + rows] - here, (rows, lanes))
        after = jnp.broadcast_to(stop - here, (rows, lanes))
        for k in range(k_lo, k_hi):
            ok = (k - half >= before) if k <= half else (k - half < after)
            for lo in range(0, chans, lanes):
                wm[k, :, lo : lo + lanes] = jnp.where(ok, convw[k : k + 1, lo : lo + lanes], 0.0)

    for way in (0, 1):
        got_1(crit, r_a1, way, reach)
        stage_2(crit, s_a2, r_a2, way, reach)
        cross(reach if way == 0 else -reach)
    rest_stage(1)
    for k in range(reach - 1, 0, -1):
        for way in (0, 1):
            got_1(crit, r_a1, way, k)
            cross(k if way == 0 else -k)
    recv(logd.at[0], r_l.at[0])
    recv(logd.at[2], r_l.at[1])
    piece_cumul()
    for j in range(1, nz // 2 - reach + 1):
        for way in (0, 1):
            if j <= nz // 2 - reach - way:
                got_2(crit, r_a2, way, j, reach)
                cross(reach + j if way == 0 else -(reach + j))
    rest_cross(0)
    rest_step(1)
    keeps[z] = keep_own[...]
    for d in ring(nz):
        send(keep_own, keeps.at[z], s_k.at[d], r_k.at[d], at(y, turn(z, d, nz)))
    for h in range(heads):
        piece_mix(h)
    recv(frames.at[0:EDGE], r_f.at[0])
    recv(frames.at[rows + EDGE : wide], r_f.at[1])
    for off in range(nz):
        for d in range(1, ny):
            recv(w.at[turn(y, -d, ny), turn(z, -off, nz), crit], r_ay.at[off, d])

    def weight(lo, count):
        return jnp.concatenate(
            [w[:, :, lo + i].reshape(width, 128) for i in range(count)], axis=1
        )

    bs[...] = nn(frames[...], weight(2, 1)).astype(BF16)
    xb = nn(frames[...], weight(0, 2)).astype(BF16)
    xs[...] = xb
    weighted = (xb[0:rows].astype(F32) * tail[...]).astype(BF16)
    state = tn(bs[0:rows], weighted).astype(BF16)
    share = local.shape[1]
    each = nz * 128 // chans
    for lo in range(chans // 128):
        local[lo * each : (lo + 1) * each] = state[:, lo * 128 : lo * 128 + 128].reshape(
            each, share, 128
        )
    mark = len(pending)
    for d in ring(nz):
        zz = turn(z, d, nz)
        send(local.at[zz], got.at[z], s_s.at[d], r_s.at[d], at(y, zz))
    got[z] = local[z]

    rest_step(2)
    for k in range(0, taps, 4):
        piece_taps(k, min(k + 4, taps))
    rest_step(3)

    for d in range(1, nz):
        recv(keeps.at[turn(z, -d, nz)], r_k.at[d])
    drain(mark)

    for d in range(1, nz):
        zz = turn(z, -d, nz)
        recv(got.at[zz], r_s.at[d])
    carry = jnp.zeros((share, 128), F32)
    decay = jnp.ones((1, 128), F32)
    for zz in range(nz):
        pref[zz] = carry
        ckeep[zz] = decay
        line = keeps[zz]
        keep = line[:, 0:128]
        for lo in range(1, chans // 128):
            keep = jnp.where(lax.div(z, each) == lo, line[:, lo * 128 : lo * 128 + 128], keep)
        carry = carry * keep + got[zz].astype(F32)
        decay = decay * keep
    tot[0:share] = carry
    tot[share : share + 8] = jnp.broadcast_to(decay, (8, 128))
    for d in ring(ny):
        send(tot, tots.at[d - 1], s_t.at[d - 1], r_t.at[d - 1], at(turn(y, d, ny), z))
    rest_step(4)
    for d in range(1, ny):
        recv(tots.at[d - 1], r_t.at[d - 1])
    come = jnp.zeros((share, 128), F32)
    for d in range(ny - 1, 0, -1):
        new = come * tots[d - 1, share : share + 1] + tots[d - 1, 0:share]
        come = jnp.where(y >= d, new, 0.0)
    for zz in range(nz):
        back[zz] = (pref[zz] + ckeep[zz] * come).astype(BF16)
    mark = len(pending)
    for d in ring(nz):
        zz = turn(z, d, nz)
        send(back.at[zz], entry.at[z], s_p.at[d], r_p.at[d], at(y, zz))
    entry[z] = back[z]

    for off in range(nz):
        for d in range(1, ny):
            recv(w.at[turn(y, -d, ny), turn(z, -off, nz), rest], r_by.at[off, d])
    cs[...] = nn(frames[...], weight(3, 1)).astype(BF16)
    scores = nt(cs[...], bs[...])
    lane_head = lax.div(iota((wide, chans), 1), PS)
    acc = jnp.zeros((wide, chans), F32)
    for h in range(heads):
        only = jnp.where(lane_head == h, xs[...].astype(F32), 0.0).astype(BF16)
        acc = acc + nn((mix[h] * scores).astype(BF16), only)
    inner[...] = acc
    zr = nn(frames[...], weight(4, 2)).astype(BF16).astype(F32)
    zs[...] = zr * jax.nn.sigmoid(zr) * gain[...]
    same = lax.div(iota((chans, chans), 0), PS) == lax.div(iota((chans, chans), 1), PS)
    block = jnp.where(same, 1.0 / PS, 0.0).astype(BF16)
    drain(mark)

    for d in range(1, nz):
        recv(entry.at[turn(z, -d, nz)], r_p.at[d])
    come_in = jnp.concatenate(
        [entry[lo * each : (lo + 1) * each].reshape(states, 128) for lo in range(chans // 128)],
        axis=1,
    )
    ssd = inner[...] + nn(cs[...], come_in) * growth[...]
    mean = nn((ssd * ssd).astype(BF16), block)
    g = (ssd * lax.rsqrt(mean + 1e-05) * zs[...]).astype(BF16)
    ext[...] = g.astype(F32)

    cols = width // (2 * nx)
    span = rows // parts
    per = cols // depth

    def conv(lo, hi):
        acc = jnp.zeros((hi - lo, chans), F32)
        for k in range(taps):
            off = EDGE - half + k
            acc = acc + wm[k, lo:hi, :] * ext[lo + off : hi + off, :]
        act[lo:hi] = (acc * jax.nn.sigmoid(acc)).astype(BF16)

    ow = weight(6, 2)
    for p in range(parts):
        for lo in range(p * span, (p + 1) * span, 32):
            conv(lo, lo + 32)
        rows_p = act[p * span : (p + 1) * span]
        for j in range(2 * nx):
            part[p, j // 2, j % 2] = nt(rows_p, ow[j * cols : (j + 1) * cols]).astype(BF16)
        send(part.at[p, :, 1 - core], pair.at[p], s_c.at[p], r_c.at[p], {"head": 2 * x + 1 - core})
    for p in range(parts):
        recv(pair.at[p], r_c.at[p])
        for d in ring(nx):
            xx = turn(x, d, nx)
            red[p, d - 1] = (part[p, xx, core].astype(F32) + pair[p, xx].astype(F32)).astype(BF16)
            send(red.at[p, d - 1], redin.at[p, d - 1], s_x.at[p, d - 1], r_x.at[p, d - 1],
                 {"head": 2 * xx + core})
    for p in range(parts):
        res = part[p, x, core].astype(F32) + pair[p, x].astype(F32)
        for d in range(1, nx):
            recv(redin.at[p, d - 1], r_x.at[p, d - 1])
            res = res + redin[p, d - 1].astype(F32)
        out[p * span : (p + 1) * span] = res.astype(BF16)
    drain(len(pending))


def solution(mesh):
    tms, groups = mesh.shape["tm"], mesh.shape["head"]
    ny, nz, nx = NY, tms // NY, groups // 2

    def local(frames, xw, zw, bcw, logd, gain, convw, outw, lens):
        rows, width = frames.shape
        depth, chans = xw.shape
        states = bcw.shape[1] // 2
        heads = logd.shape[0]
        taps = convw.shape[0]
        share = states * chans // (nz * 128)
        cols = width // groups
        wide = rows + 2 * EDGE
        parts = 8
        dma = pltpu.SemaphoreType.DMA
        v = pltpu.VMEM
        others = max(nx - 1, 1)
        scratch = [
            pltpu.SMEM(lens.shape, jnp.int32),
            v((ny, nz, 8, depth, 128), BF16),
            v((wide, width), BF16),
            v((3, heads, rows), F32),
            v((1, chans), F32),
            v((taps, chans), F32),
            v((heads, wide, wide), F32),
            v((wide, chans), F32),
            v((rows, chans), F32),
            v((taps, rows, chans), F32),
            v((wide, chans), BF16),
            v((wide, states), BF16),
            v((wide, states), BF16),
            v((wide, chans), F32),
            v((wide, chans), F32),
            v((nz, share, 128), BF16),
            v((nz, share, 128), BF16),
            v((nz, 1, chans), F32),
            v((1, chans), F32),
            v((nz, share, 128), F32),
            v((nz, 1, 128), F32),
            v((share + 8, 128), F32),
            v((ny - 1, share + 8, 128), F32),
            v((nz, share, 128), BF16),
            v((nz, share, 128), BF16),
            v((wide, chans), F32),
            v((rows, chans), BF16),
            v((parts, nx, 2, rows // parts, cols), BF16),
            v((parts, nx, rows // parts, cols), BF16),
            v((parts, others, rows // parts, cols), BF16),
            v((parts, others, rows // parts, cols), BF16),
            dma((13,)),
            dma((2, nz // 2 + 1)), dma((2, nz // 2 + 1)),
            dma((2, nz // 2 + 1)), dma((2, nz // 2 + 1)),
            dma((nz, ny)), dma((nz, ny)),
            dma((2, nz // 2 + 1)), dma((2, nz // 2 + 1)),
            dma((nz, ny)), dma((nz, ny)),
            dma((2,)), dma((2,)),
            dma((2,)), dma((2,)),
            dma((nz,)), dma((nz,)),
            dma((nz,)), dma((nz,)),
            dma((ny - 1,)), dma((ny - 1,)),
            dma((nz,)), dma((nz,)),
            dma((parts,)), dma((parts,)),
            dma((parts, others)), dma((parts, others)),
        ]
        hbm = pl.BlockSpec(memory_space=pltpu.HBM)
        return pl.pallas_call(
            functools.partial(kernel, ny, nz, nx, parts),
            out_shape=jax.ShapeDtypeStruct((rows, cols), BF16),
            in_specs=[hbm] * 9,
            out_specs=pl.BlockSpec(memory_space=pltpu.VMEM),
            scratch_shapes=scratch,
            compiler_params=pltpu.CompilerParams(
                collective_id=0, has_side_effects=True, vmem_limit_bytes=28 * 2**20
            ),
            name="mixer",
        )(*[
            pltpu.with_memory_space_constraint(v, pltpu.HBM)
            for v in (lens, frames, xw, zw, bcw, logd, gain.reshape(1, chans), convw, outw.T)
        ])

    in_specs = (
        P("tm", None), P("tm", "head"), P("tm", "head"), P("tm", None), P("head", "tm"),
        P("head"), P(None, "head"), P("head", "tm"), P(),
    )
    return jax.shard_map(
        local, mesh=mesh, in_specs=in_specs, out_specs=P("tm", "head"), check_vma=False
    )
```
